256 devices in a mesh: section: 32 (over z_lo, y, x), tp: 8 (over z_hi, core).
Axes of the slice: x: 4, y: 4, z: 8 (z_hi: 4, z_lo: 2; z = z_hi * 2 + z_lo), core: 2. Of those that a mesh axis runs over, the one named last changes fastest.
Arguments:
- prefill_hidden: bfloat16 [8192, 8192], P('section', 'tp'), may hold values from -180 to 180
- norm_gain: float32 [8192], replicated, may hold values from 0.25 to 1.75
- key_weight: bfloat16 [8192, 1024], P(None, 'tp'), may hold values from -0.0625 to 0.0625
- value_weight: bfloat16 [8192, 1024], P(None, 'tp'), may hold values from -0.0625 to 0.0625
- prefill_query: bfloat16 [8192, 8192], P('section', 'tp'), may hold values from -102 to 102
- resident_keys: bfloat16 [8192, 16, 1024], P('section', None, 'tp'), may hold values from -6 to 6
- resident_values: bfloat16 [8192, 16, 1024], P('section', None, 'tp'), may hold values from -6 to 6
- decode_query: bfloat16 [512, 8192], P('section', 'tp'), may hold values from -102 to 102
- page_owner: int32 [512], P('section'), may hold values from 0 to 31, as said below
- block_table: int32 [512, 64], P('section'), may hold values from 0 to 319, as said below
- context_len: int32 [512], P('section'), may hold values from 1 to 1024, as said below
Outputs:
- prefill_attention: bfloat16 [8192, 8192], P('section', 'tp')
- decode_attention: bfloat16 [512, 8192], P('section', 'tp')
The draws below stay inside these ranges and needn't reach their ends.
Inputs may be any that keep to these rules, and one draw needn't show every extreme that they name: `page_owner`: the 16 pages of each section device go to 8 different owners, exactly 2 pages to each; one owner receives pages from every section device. `block_table`: row entries name first the row's resident pages (below 256), then 256 + page_slot for at most 4 pages sent to the row's owner; every page sent to an owner is named by exactly one of its rows; entries after a row's pages are 0. `context_len`: A row's last visible token lies in the last page its table names.
All inputs are finite; a program needn't handle non-finite values.
Results may differ from the reference program's by a relative error of at most 0.011.
Values may be sent and summed in bfloat16 or wider, within the bound.
A program may use at most 192 MiB of HBM per device.

```python
import math
import jax
import jax.numpy as jnp
from jax import lax

D = 8192
HQ = 64
KVH = 8
HD = 128
PAGE = 16
CAP = 2
RES_ROW = 60
B_DEV = 16
SEQ = 8192
PAGES_DEV = 16
INC = 64
INC_ROW = 4
MAXP = 64
POOL = 256
ROWS = 512
N_SECTION = 32


def routing_plan(key):
    plan_keys = jax.random.split(jax.random.fold_in(key, 7101), 8)
    owner_ids = jnp.arange(N_SECTION, dtype=jnp.int32)
    picks_each = PAGES_DEV // CAP
    hottest = jax.random.randint(plan_keys[0], (), 0, N_SECTION)
    ranking = jnp.argsort(jax.random.permutation(plan_keys[1], N_SECTION), stable=True).astype(jnp.int32)
    noise = jax.random.randint(plan_keys[2], (N_SECTION, N_SECTION), 0, 2 * N_SECTION)
    favour = 3 * (N_SECTION - ranking)[None, :]
    favour = favour + 100000 * (owner_ids[None, :] == hottest).astype(jnp.int32)
    favour = favour + 50000 * (owner_ids[None, :] == owner_ids[:, None]).astype(jnp.int32)
    priority = (noise + favour) * N_SECTION + owner_ids[None, :]
    chosen = lax.top_k(priority, picks_each)[1].astype(jnp.int32)
    page_keys = jax.random.split(plan_keys[3], N_SECTION)
    shuffled = jax.vmap(lambda one_key: jax.random.permutation(one_key, PAGES_DEV))(page_keys).astype(jnp.int32)
    owners = jnp.take_along_axis(chosen, shuffled // CAP, axis=1)
    picked = jnp.sum((chosen[:, :, None] == owner_ids[None, None, :]).astype(jnp.int32), axis=1)
    return (owners, picked, hottest, plan_keys)


def decode_plan(key):
    owners, picked, hottest, plan_keys = routing_plan(key)
    owner_ids = jnp.arange(N_SECTION, dtype=jnp.int32)
    row_ids = jnp.arange(B_DEV, dtype=jnp.int32)
    filled = jnp.sum(picked, axis=0) * CAP
    source_order = jnp.argsort(1 - jnp.transpose(picked), axis=1, stable=True).astype(jnp.int32)
    entry_index = row_ids[:, None] + B_DEV * jnp.arange(INC_ROW, dtype=jnp.int32)[None, :]
    source_of = source_order[:, jnp.minimum(entry_index // CAP, N_SECTION - 1)]
    slot_of = source_of * CAP + (entry_index % CAP)[None, :, :]
    live_entry = entry_index[None, :, :] < filled[:, None, None]
    incoming_count = jnp.sum(live_entry.astype(jnp.int32), axis=2)
    hot_row = (owner_ids[:, None] == hottest) & (row_ids[None, :] == 0)
    resident_count = jnp.where(hot_row, RES_ROW, jax.random.randint(plan_keys[4], (N_SECTION, B_DEV), 1, RES_ROW + 1))
    resident_pick = jax.random.randint(plan_keys[5], (N_SECTION, B_DEV, MAXP), 0, POOL)
    column_ids = jnp.arange(MAXP, dtype=jnp.int32)[None, None, :]
    incoming_pos = column_ids - resident_count[:, :, None]
    incoming_slot = jnp.take_along_axis(slot_of, jnp.clip(incoming_pos, 0, INC_ROW - 1), axis=2)
    table_rows = jnp.where(column_ids < resident_count[:, :, None], resident_pick, jnp.where(incoming_pos < incoming_count[:, :, None], POOL + incoming_slot, 0))
    trimmed = jnp.where(hot_row, 0, jax.random.randint(plan_keys[6], (N_SECTION, B_DEV), 0, PAGE))
    row_length = PAGE * (resident_count + incoming_count) - trimmed
    return (table_rows.reshape(N_SECTION * B_DEV, MAXP).astype(jnp.int32), row_length.reshape(N_SECTION * B_DEV).astype(jnp.int32))


def draw_page_owner(key, part):
    return routing_plan(key)[0].reshape(N_SECTION * PAGES_DEV).astype(jnp.int32)


def draw_block_table(key, part):
    return decode_plan(key)[0]


def draw_context_len(key, part):
    return decode_plan(key)[1]


def query_values(key, salt, row_count):
    draw_keys = jax.random.split(jax.random.fold_in(key, salt), 1)
    return jnp.clip(2.5 * jax.random.normal(draw_keys[0], (row_count, HQ * HD), jnp.float32), -12.0, 12.0)


def draw_prefill_query(key, part):
    return query_values(key, 4409, SEQ).astype(jnp.bfloat16)


def draw_decode_query(key, part):
    return query_values(key, 5519, ROWS).astype(jnp.bfloat16)


def draw_prefill_hidden(key, part):
    draw_keys = jax.random.split(jax.random.fold_in(key, 2203), 3)
    row_scale = jnp.exp(jax.random.uniform(draw_keys[1], (SEQ, 1), jnp.float32, 0.0, math.log(10.0)))
    column_scale = jnp.exp(jax.random.uniform(draw_keys[2], (1, D), jnp.float32, math.log(0.3), math.log(3.0)))
    base_values = jnp.clip(jax.random.normal(draw_keys[0], (SEQ, D), jnp.float32), -6.0, 6.0)
    return (base_values * row_scale * column_scale).astype(jnp.bfloat16)


def levels(rng, dims, shards, smallest, largest):
    def one(position, shards_of):
        heights = jax.random.uniform(jax.random.fold_in(jax.random.fold_in(rng, 6), position), (shards_of,), jnp.float32, smallest / len(shards), largest / len(shards))
        return jnp.repeat(jnp.exp(heights), dims[position] // shards_of).reshape((-1,) + (1,) * (len(dims) - position - 1))

    level = one(*shards[0])
    for cut in shards[1:]:
        level = level * one(*cut)
    return level


def gaussian(stream_key, shape, width, most, cuts=(), held_as=jnp.bfloat16):
    result = width * jax.random.normal(stream_key, shape, jnp.float32)
    if cuts:
        result = result * levels(stream_key, shape, cuts, -0.22, 0.18)
    return jnp.clip(result, -most, most).astype(held_as)


def setup_inputs(seed: int = 0) -> dict:
    seeds = jax.random.split(jax.random.key(seed), 12)
    prefill_hidden = draw_prefill_hidden(jax.random.fold_in(seeds[11], 71), 0)
    norm_gain = jnp.clip(1.0 + 0.15 * jax.random.normal(seeds[1], (D,), jnp.float32), 0.25, 1.75)
    key_weight = gaussian(seeds[2], (D, KVH * HD), D ** -0.5, 0.0625, ((1, 8),))
    value_weight = gaussian(seeds[3], (D, KVH * HD), D ** -0.5, 0.0625, ((1, 8),))
    prefill_query = draw_prefill_query(jax.random.fold_in(seeds[11], 71), 0)
    resident_keys = gaussian(seeds[5], (N_SECTION * POOL, PAGE, KVH * HD), 1.0, 6.0, ((0, 32), (2, 8)))
    resident_values = gaussian(seeds[6], (N_SECTION * POOL, PAGE, KVH * HD), 1.0, 6.0, ((0, 32), (2, 8)))
    decode_query = draw_decode_query(jax.random.fold_in(seeds[11], 71), 0)
    page_owner = draw_page_owner(jax.random.fold_in(seeds[11], 71), 0)
    block_table = draw_block_table(jax.random.fold_in(seeds[11], 71), 0)
    context_len = draw_context_len(jax.random.fold_in(seeds[11], 71), 0)
    return {"prefill_hidden": prefill_hidden, "norm_gain": norm_gain, "key_weight": key_weight, "value_weight": value_weight, "prefill_query": prefill_query, "resident_keys": resident_keys, "resident_values": resident_values, "decode_query": decode_query, "page_owner": page_owner, "block_table": block_table, "context_len": context_len}


NORM_EPSILON = 1e-05
ROPE_THETA = 500000.0

def rotate_keys(raw_keys, positions):
    head_width = raw_keys.shape[-1]
    half_width = head_width // 2
    frequency = jnp.exp(jnp.arange(half_width, dtype=jnp.float32) * (-2.0 * math.log(ROPE_THETA) / head_width))
    angles = positions.astype(jnp.float32)[:, None] * frequency[None, :]
    cosine = jnp.cos(angles)[:, None, :]
    sine_part = jnp.sin(angles)[:, None, :]
    first_half = raw_keys[..., :half_width]
    second_half = raw_keys[..., half_width:]
    return jnp.concatenate([first_half * cosine - second_half * sine_part, second_half * cosine + first_half * sine_part], axis=-1)

def reference(prefill_hidden, norm_gain, key_weight, value_weight, prefill_query, resident_keys, resident_values, decode_query, page_owner, block_table, context_len):
    seq_rows = prefill_hidden.shape[0]
    key_width = KVH * HD
    group_size = HQ // KVH
    score_scale = 1.0 / math.sqrt(HD)
    hidden_f32 = prefill_hidden.astype(jnp.float32)
    inverse_rms = lax.rsqrt(lax.optimization_barrier(jnp.mean(hidden_f32 * hidden_f32, axis=1, keepdims=True)) + NORM_EPSILON)
    normed = (hidden_f32 * inverse_rms * norm_gain.astype(jnp.float32)).astype(jnp.bfloat16)
    raw_keys = jnp.dot(normed, key_weight, preferred_element_type=jnp.float32)
    value_rows = jnp.dot(normed, value_weight, preferred_element_type=jnp.float32).astype(jnp.bfloat16)
    positions = jnp.arange(seq_rows, dtype=jnp.int32)
    key_rows = rotate_keys(raw_keys.reshape(seq_rows, KVH, HD), positions).reshape(seq_rows, key_width).astype(jnp.bfloat16)
    block_rows = math.gcd(seq_rows, 128)
    key_f32 = key_rows.astype(jnp.float32).reshape(seq_rows, KVH, HD)
    value_f32 = value_rows.astype(jnp.float32).reshape(seq_rows, KVH, HD)
    query_blocks = prefill_query.reshape(seq_rows // block_rows, block_rows, KVH, group_size, HD)
    block_starts = jnp.arange(seq_rows // block_rows, dtype=jnp.int32) * block_rows

    def prefill_block(inputs):
        query_block, first_row = inputs
        query_pos = first_row + jnp.arange(block_rows, dtype=jnp.int32)
        scores = jnp.einsum('tkgd,rkd->kgtr', query_block.astype(jnp.float32), key_f32) * score_scale
        visible = positions[None, :] <= query_pos[:, None]
        scores = jnp.where(visible, scores, -jnp.inf)
        row_max = lax.optimization_barrier(jnp.max(scores, axis=-1, keepdims=True))
        weights = jnp.exp(scores - row_max)
        row_sum = lax.optimization_barrier(jnp.sum(weights, axis=-1, keepdims=True))
        rounded = lax.optimization_barrier(weights.astype(jnp.bfloat16)).astype(jnp.float32)
        attended = jnp.einsum('kgtr,rkd->kgtd', rounded, value_f32) / row_sum
        return jnp.transpose(attended, (2, 0, 1, 3)).reshape(block_rows, HQ * HD).astype(jnp.bfloat16)
    prefill_attention = lax.map(prefill_block, (query_blocks, block_starts)).reshape(seq_rows, HQ * HD)
    sections = N_SECTION
    pages_total = seq_rows // PAGE
    pages_each = pages_total // sections
    page_data = jnp.concatenate([key_rows, value_rows], axis=1).reshape(pages_total, PAGE, 2 * key_width)
    owners = page_owner.reshape(sections, pages_each)
    page_index = jnp.arange(pages_each, dtype=jnp.int32)
    earlier = (owners[:, :, None] == owners[:, None, :]) & (page_index[None, None, :] < page_index[None, :, None])
    page_rank = lax.optimization_barrier(jnp.sum(earlier.astype(jnp.int32), axis=2))
    source_section = jnp.arange(sections, dtype=jnp.int32)[:, None]
    target = (owners * INC + source_section * CAP + page_rank).reshape(pages_total).astype(jnp.int32)
    incoming = jnp.zeros((sections * INC, PAGE, 2 * key_width), jnp.bfloat16).at[target].set(page_data)
    incoming = incoming.reshape(sections, INC, PAGE, 2 * key_width)
    cache_keys = jnp.concatenate([resident_keys.reshape(sections, POOL, PAGE, key_width), incoming[..., :key_width]], axis=1)
    cache_values = jnp.concatenate([resident_values.reshape(sections, POOL, PAGE, key_width), incoming[..., key_width:]], axis=1)
    tables = block_table.reshape(sections, B_DEV, MAXP)
    lengths = context_len.reshape(sections, B_DEV)
    queries = decode_query.reshape(sections, B_DEV, KVH, group_size, HD)
    key_span = MAXP * PAGE

    def decode_group(inputs):
        group_keys, group_values, table_rows, length_rows, query_rows = inputs
        gathered_keys = group_keys[table_rows].reshape(B_DEV, key_span, KVH, HD).astype(jnp.float32)
        gathered_values = group_values[table_rows].reshape(B_DEV, key_span, KVH, HD).astype(jnp.float32)
        scores = jnp.einsum('bkgd,blkd->bkgl', query_rows.astype(jnp.float32), gathered_keys) * score_scale
        visible = (jnp.arange(key_span, dtype=jnp.int32)[None, :] < length_rows[:, None])[:, None, None, :]
        scores = jnp.where(visible, scores, -jnp.inf)
        row_max = lax.optimization_barrier(jnp.max(scores, axis=-1, keepdims=True))
        weights = jnp.exp(scores - row_max)
        row_sum = lax.optimization_barrier(jnp.sum(weights, axis=-1, keepdims=True))
        rounded = lax.optimization_barrier(weights.astype(jnp.bfloat16)).astype(jnp.float32)
        attended = jnp.einsum('bkgl,blkd->bkgd', rounded, gathered_values) / row_sum
        return attended.reshape(B_DEV, HQ * HD).astype(jnp.bfloat16)
    decode_attention = lax.map(decode_group, (cache_keys, cache_values, tables, lengths, queries)).reshape(ROWS, HQ * HD)
    return (prefill_attention, decode_attention)
```

```python
import functools
import math

import numpy as np

import jax
import jax.numpy as jnp
from jax import lax
from jax.experimental import pallas as pl
from jax.experimental.pallas import tpu as pltpu
from jax.sharding import PartitionSpec as P

MESH = pl.DeviceIdType.MESH
HD = 128
PAGE = 16
NORM_EPSILON = 1e-05
ROPE_THETA = 500000.0
NEG = -1e30
CHUNKS = 4
TILE_Y = 4
UNIT_HEADS = 2
N_COPIES = 26
N_META = 9
POW = math.log2(math.e) / math.sqrt(HD)

NT = (((1,), (1,)), ((), ()))
TN = (((0,), (0,)), ((), ()))


def rope_tables(stretch, sections):
    half = HD // 2
    exponent = np.arange(half, dtype=np.float32) * np.float32(-2.0 * math.log(ROPE_THETA) / HD)
    frequency = np.exp(exponent).astype(np.float64)
    inner = np.arange(stretch)[:, None] * frequency[None, :]
    outer = (np.arange(sections) * stretch)[:, None] * frequency[None, :]

    def both(angles):
        cosine = np.concatenate([np.cos(angles), np.cos(angles)], axis=1)
        sine = np.concatenate([np.sin(angles), np.sin(angles)], axis=1)
        return cosine.astype(np.float32), sine.astype(np.float32)

    return both(inner) + both(outer)


def kernel(
    hidden,
    gain,
    key_weight,
    value_weight,
    query,
    resident_keys,
    resident_values,
    decode_query,
    owner,
    table,
    context,
    cos_in,
    sin_in,
    cos_out,
    sin_out,
    out,
    decode_out,
    hid,
    wkv,
    kb,
    vb,
    meta,
    qs,
    rk,
    rv,
    dqm,
    cosine,
    sine,
    row_max,
    row_sum,
    acc,
    visible_pages,
    last_page,
    count_full,
    count_last,
    dec_max,
    dec_sum,
    dec_acc,
    local_sem,
    send_sem,
    recv_sem,
    meta_send,
    meta_recv,
):
    stretch = hidden.shape[0]
    width = hidden.shape[1]
    chunks = kb.shape[0]
    rows = stretch // chunks
    half_rows = rows // 2
    heads = qs.shape[0]
    pages_chunk = rows // PAGE
    pages_here = stretch // PAGE
    pool = rk.shape[0]
    max_pages = table.shape[1]
    decode_rows = decode_query.shape[0]
    lanes = 128

    s = lax.axis_index("section")
    t = lax.axis_index("tp")
    zh, core = t // 2, t % 2
    zl, y, x = s // 16, (s // 4) % 4, s % 4
    t_r, t_l, t_o = ((zh + 1) % 4) * 2 + core, ((zh + 3) % 4) * 2 + core, ((zh + 2) % 4) * 2 + core
    other = 1 - core
    t_p = zh * 2 + other
    p_r, p_l, p_o = ((zh + 1) % 4) * 2 + other, ((zh + 3) % 4) * 2 + other, ((zh + 2) % 4) * 2 + other
    xp, xm, xo = (x + 1) % 4, (x + 3) % 4, (x + 2) % 4
    yp, ym, yo = (y + 1) % 4, (y + 3) % 4, (y + 2) % 4
    zo = 1 - zl

    def at_section(zz, yy, xx):
        return (zz * 16 + yy * 4 + xx, t)

    z_right, z_left, partner = (s, t_r), (s, t_l), (s, t_p)
    z_other = at_section(zo, y, x)
    x_right, x_left = at_section(zl, y, xp), at_section(zl, y, xm)
    y_up, y_down = at_section(zl, yp, x), at_section(zl, ym, x)

    every = slice(None)

    def routes(c):
        top, bottom = pl.ds(0, half_rows), pl.ds(half_rows, half_rows)
        mine = hidden.at[pl.ds(pl.multiple_of(c * rows, rows), rows), :]
        return (
            (mine, hid.at[c, t], hid.at[c, t_l], z_right),
            (mine, hid.at[c, t], hid.at[c, t_r], z_left),
            (hid.at[c, t_l, top], hid.at[c, t_l, top], hid.at[c, t_o, top], z_right),
            (hid.at[c, t_r, bottom], hid.at[c, t_r, bottom], hid.at[c, t_o, bottom], z_left),
            (mine, hid.at[c, t], hid.at[c, t_p], partner),
            (hid.at[c, t_l], hid.at[c, t_l], hid.at[c, p_l], partner),
            (hid.at[c, t_r], hid.at[c, t_r], hid.at[c, p_r], partner),
            (hid.at[c, t_o], hid.at[c, t_o], hid.at[c, p_o], partner),
            (kb.at[c, zl, y, x], kb.at[c, zl, y, x], kb.at[c, zo, y, x], z_other),
            (vb.at[c, zl, y, x], vb.at[c, zl, y, x], vb.at[c, zo, y, x], z_other),
            (kb.at[c, :, y, x], kb.at[c, :, y, x], kb.at[c, :, y, xm], x_right),
            (kb.at[c, :, y, x], kb.at[c, :, y, x], kb.at[c, :, y, xp], x_left),
            (vb.at[c, :, y, x], vb.at[c, :, y, x], vb.at[c, :, ym, x], y_up),
            (vb.at[c, :, y, x], vb.at[c, :, y, x], vb.at[c, :, yp, x], y_down),
            (kb.at[c, 0, y, xm], kb.at[c, 0, y, xm], kb.at[c, 0, y, xo], x_right),
            (kb.at[c, 1, y, xp], kb.at[c, 1, y, xp], kb.at[c, 1, y, xo], x_left),
            (vb.at[c, 0, ym, x], vb.at[c, 0, ym, x], vb.at[c, 0, yo, x], y_up),
            (vb.at[c, 1, yp, x], vb.at[c, 1, yp, x], vb.at[c, 1, yo, x], y_down),
            (kb.at[c, :, y], kb.at[c, :, y], kb.at[c, :, ym], y_up),
            (kb.at[c, :, y], kb.at[c, :, y], kb.at[c, :, yp], y_down),
            (vb.at[c, :, :, x], vb.at[c, :, :, x], vb.at[c, :, :, xm], x_right),
            (vb.at[c, :, :, x], vb.at[c, :, :, x], vb.at[c, :, :, xp], x_left),
            (kb.at[c, 0, ym], kb.at[c, 0, ym], kb.at[c, 0, yo], y_up),
            (kb.at[c, 1, yp], kb.at[c, 1, yp], kb.at[c, 1, yo], y_down),
            (vb.at[c, 0, :, xm], vb.at[c, 0, :, xm], vb.at[c, 0, :, xo], x_right),
            (vb.at[c, 1, :, xp], vb.at[c, 1, :, xp], vb.at[c, 1, :, xo], x_left),
        )

    meta_routes = (
        (meta.at[zl, y, x], meta.at[zo, y, x], z_other),
        (meta.at[:, y, x], meta.at[:, y, xm], x_right),
        (meta.at[:, y, x], meta.at[:, y, xp], x_left),
        (meta.at[0, y, xm], meta.at[0, y, xo], x_right),
        (meta.at[1, y, xp], meta.at[1, y, xo], x_left),
        (meta.at[:, y], meta.at[:, ym], y_up),
        (meta.at[:, y], meta.at[:, yp], y_down),
        (meta.at[0, ym], meta.at[0, yo], y_up),
        (meta.at[1, yp], meta.at[1, yo], y_down),
    )

    def remote(c, k):
        source, target, _, device = routes(c)[k]
        return pltpu.make_async_remote_copy(
            src_ref=source,
            dst_ref=target,
            send_sem=send_sem.at[c, k],
            recv_sem=recv_sem.at[c, k],
            device_id=device,
            device_id_type=MESH,
        )

    def arrival(c, k):
        _, _, landing, device = routes(c)[k]
        return pltpu.make_async_remote_copy(
            src_ref=landing,
            dst_ref=landing,
            send_sem=send_sem.at[c, k],
            recv_sem=recv_sem.at[c, k],
            device_id=device,
            device_id_type=MESH,
        )

    def start(c, *ks):
        for k in ks:
            remote(c, k).start()

    def await_arrival(c, *ks):
        for k in ks:
            arrival(c, k).wait_recv()

    def meta_copy(k):
        source, _, device = meta_routes[k]
        return pltpu.make_async_remote_copy(
            src_ref=source,
            dst_ref=source,
            send_sem=meta_send.at[k],
            recv_sem=meta_recv.at[k],
            device_id=device,
            device_id_type=MESH,
        )

    def meta_arrival(k):
        _, landing, device = meta_routes[k]
        return pltpu.make_async_remote_copy(
            src_ref=landing,
            dst_ref=landing,
            send_sem=meta_send.at[k],
            recv_sem=meta_recv.at[k],
            device_id=device,
            device_id_type=MESH,
        )

    def meta_start(*ks):
        for k in ks:
            meta_copy(k).start()

    def meta_await(*ks):
        for k in ks:
            meta_arrival(k).wait_recv()

    own_hidden = [
        pltpu.make_async_copy(
            hidden.at[pl.ds(c * rows, rows), :], hid.at[c, t], local_sem.at[c]
        )
        for c in range(chunks)
    ]
    weights_in = [
        pltpu.make_async_copy(key_weight, wkv.at[:, pl.ds(0, lanes)], local_sem.at[chunks]),
        pltpu.make_async_copy(value_weight, wkv.at[:, pl.ds(lanes, lanes)], local_sem.at[chunks + 1]),
    ]
    resident_in = [
        pltpu.make_async_copy(resident_keys, rk, local_sem.at[chunks + 2]),
        pltpu.make_async_copy(resident_values, rv, local_sem.at[chunks + 3]),
    ]
    query_in = [
        pltpu.make_async_copy(
            query.at[:, pl.ds(h * lanes, lanes)], qs.at[h], local_sem.at[chunks + 4 + h]
        )
        for h in range(heads)
    ]

    neighbours = (z_right, z_left, partner, z_other, x_right, x_left, y_up, y_down)
    barrier = pltpu.get_barrier_semaphore()
    for device in neighbours:
        pl.semaphore_signal(barrier, inc=1, device_id=device, device_id_type=MESH)
    for copy in own_hidden + resident_in + weights_in + query_in:
        copy.start()
    pl.semaphore_wait(barrier, len(neighbours))

    for c in range(2):
        start(c, 0, 1, 4)

    owners = [owner[i] for i in range(pages_here)]
    page_row = lax.broadcasted_iota(jnp.int32, (pages_here, lanes), 0)
    codes = jnp.zeros((pages_here, lanes), jnp.int32)
    for i in range(pages_here):
        rank = jnp.int32(0)
        for j in range(i):
            rank = rank + jnp.where(owners[j] == owners[i], 1, 0).astype(jnp.int32)
        code = owners[i] * 64 + s * 2 + rank
        codes = jnp.where(page_row == i, code, codes)
    meta[zl, y, x] = codes

    lane_row = lax.broadcasted_iota(jnp.int32, (1, lanes), 1) % decode_rows
    lengths = jnp.zeros((1, lanes), jnp.int32)
    for r in range(decode_rows):
        lengths = jnp.where(lane_row == r, context[r], lengths)
    full_pages = lax.shift_right_logical(lengths - 1, 4)
    last_tokens = lengths - full_pages * PAGE
    last_page[...] = jnp.zeros((1, lanes), jnp.int32)

    def table_row(j, carry):
        entries = jnp.zeros((1, lanes), jnp.int32)
        for r in range(decode_rows):
            entries = jnp.where(lane_row == r, table[r, j], entries)
        visible_pages[pl.ds(j, 1), :] = jnp.where(full_pages > j, entries, -1)
        last_page[...] = jnp.where(full_pages == j, entries, last_page[...])
        return carry

    lax.fori_loop(0, max_pages, table_row, 0)
    meta_start(0)

    for h in range(heads):
        dqm[h * decode_rows : (h + 1) * decode_rows, :] = decode_query[:, h * lanes : (h + 1) * lanes]
    ca, sa = cos_out[pl.ds(s, 1), :], sin_out[pl.ds(s, 1), :]
    low = lax.broadcasted_iota(jnp.int32, (1, lanes), 1) < lanes // 2
    cosine[...] = ca * cos_in[...] - sa * sin_in[...]
    sine[...] = jnp.where(low, -1.0, 1.0) * (sa * cos_in[...] + ca * sin_in[...])
    row_max[...] = jnp.full(row_max.shape, NEG, jnp.float32)
    row_sum[...] = jnp.zeros(row_sum.shape, jnp.float32)
    acc[...] = jnp.zeros(acc.shape, jnp.float32)
    dec_max[...] = jnp.full(dec_max.shape, NEG, jnp.float32)
    dec_sum[...] = jnp.zeros(dec_sum.shape, jnp.float32)
    dec_acc[...] = jnp.zeros(dec_acc.shape, jnp.float32)

    def count_pages(page_ids):
        def step(j, total):
            return total + jnp.where(page_ids == visible_pages[pl.ds(j, 1), :], 1.0, 0.0)

        total = lax.fori_loop(
            0, max_pages, step, jnp.zeros(page_ids.shape, jnp.float32), unroll=8
        )
        return total, jnp.where(page_ids == last_page[...], 1.0, 0.0)

    def decode_tile(keys, values, counts):
        scores = lax.dot_general(keys, dqm[...], NT, preferred_element_type=jnp.float32)
        scores = jnp.where(counts > 0.0, scores, NEG)
        old = dec_max[...]
        new = jnp.maximum(old, jnp.max(scores, axis=0, keepdims=True))
        weights = counts * jnp.exp2((scores - new) * POW)
        shrink = jnp.exp2((old - new) * POW)
        dec_max[...] = new
        dec_sum[...] = dec_sum[...] * shrink + jnp.sum(weights, axis=0, keepdims=True)
        dec_acc[...] = dec_acc[...] * shrink + lax.dot_general(
            values, weights.astype(jnp.bfloat16), TN, preferred_element_type=jnp.float32
        )

    for copy in resident_in:
        copy.wait()
    tile_pages = 32
    token_of = lax.broadcasted_iota(jnp.int32, (PAGE, lanes), 0)
    in_last = jnp.where(token_of < last_tokens, 1.0, 0.0)

    def resident_tile(i, carry):
        first = pl.multiple_of(i * tile_pages, tile_pages)
        ids = first + lax.broadcasted_iota(jnp.int32, (tile_pages, lanes), 0)
        total, last = count_pages(ids)
        counts = [
            jnp.broadcast_to(total[p : p + 1, :], (PAGE, lanes))
            + in_last * jnp.broadcast_to(last[p : p + 1, :], (PAGE, lanes))
            for p in range(tile_pages)
        ]
        decode_tile(
            rk[pl.ds(first, tile_pages)].reshape(tile_pages * PAGE, lanes),
            rv[pl.ds(first, tile_pages)].reshape(tile_pages * PAGE, lanes),
            jnp.concatenate(counts, axis=0),
        )
        return carry

    lax.fori_loop(0, pool // tile_pages, resident_tile, 0)

    def count_incoming():
        def one(i, carry):
            for yy in range(4):
                code = meta[i // 4, yy, i % 4] - s * 64
                ids = jnp.where((code >= 0) & (code < 64), code + pool, -5)
                total, last = count_pages(ids)
                sec = (i // 4) * 16 + yy * 4 + i % 4
                count_full[sec] = total
                count_last[sec] = last
            return carry

        lax.fori_loop(0, 8, one, 0)

    def decode_chunk(c):
        def one(i, carry):
            zz, yy = i // 4, i % 4
            counts = []
            for xx in range(4):
                for p in range(pages_chunk):
                    at = pl.ds(c * pages_chunk + p, 1)
                    counts.append(
                        jnp.broadcast_to(count_full[i * 4 + xx, at, :], (PAGE, lanes))
                        + in_last * jnp.broadcast_to(count_last[i * 4 + xx, at, :], (PAGE, lanes))
                    )
            decode_tile(
                kb[c, zz, yy].reshape(4 * rows, lanes),
                vb[c, zz, yy].reshape(4 * rows, lanes),
                jnp.concatenate(counts, axis=0),
            )
            return carry

        lax.fori_loop(0, 8, one, 0)

    shards = hid.shape[1]

    def project(c):
        squares = jnp.zeros((rows, 1), jnp.float32)
        for j in range(shards):
            block = hid[c, j].astype(jnp.float32)
            squares = squares + jnp.sum(block * block, axis=1, keepdims=True)
        inverse = lax.rsqrt(squares * (1.0 / (shards * width)) + NORM_EPSILON)
        total = jnp.zeros((rows, 2 * lanes), jnp.float32)
        for j in range(shards):
            block = hid[c, j].astype(jnp.float32)
            normed = (block * inverse * gain[:, j * width : (j + 1) * width]).astype(jnp.bfloat16)
            total = total + jnp.dot(
                normed, wkv[j * width : (j + 1) * width, :], preferred_element_type=jnp.float32
            )
        keys = total[:, :lanes]
        at = pl.ds(pl.multiple_of(c * rows, rows), rows)
        keys = keys * cosine[at, :] + pltpu.roll(keys, lanes // 2, 1) * sine[at, :]
        kb[c, zl, y, x] = keys.astype(jnp.bfloat16)
        vb[c, zl, y, x] = total[:, lanes:].astype(jnp.bfloat16)

    tile_sections = 4 * TILE_Y
    tile_keys = tile_sections * rows
    tiles = 32 // tile_sections
    own_tile = s // tile_sections

    def attend(c, kt, hp, masked):
        first_y = kt * TILE_Y
        keys = kb[c, first_y // 4, pl.ds(first_y % 4, TILE_Y)].reshape(tile_keys, lanes)
        values = vb[c, first_y // 4, pl.ds(first_y % 4, TILE_Y)].reshape(tile_keys, lanes)
        if masked:
            n = lax.broadcasted_iota(jnp.int32, (stretch, lanes), 1)
            query_pos = s * stretch + lax.broadcasted_iota(jnp.int32, (stretch, lanes), 0)
        for i in range(UNIT_HEADS):
            h = hp * UNIT_HEADS + i
            scores = lax.dot_general(qs[h], keys, NT, preferred_element_type=jnp.float32)
            pieces = [scores[:, j * lanes : (j + 1) * lanes] for j in range(tile_keys // lanes)]
            if masked:
                for j in range(len(pieces)):
                    at = j * lanes + n
                    key_pos = (kt * tile_sections + at // rows) * stretch + c * rows + at % rows
                    pieces[j] = jnp.where(key_pos <= query_pos, pieces[j], NEG)
            top = functools.reduce(jnp.maximum, pieces)
            old = row_max[h]
            new = jnp.maximum(old, jnp.max(top, axis=1, keepdims=True))
            shrink = jnp.exp2((old - new) * POW)
            weights = [jnp.exp2((piece - new) * POW) for piece in pieces]
            row_max[h] = new
            row_sum[h] = row_sum[h] * shrink + functools.reduce(jnp.add, weights)
            weights = jnp.concatenate([w.astype(jnp.bfloat16) for w in weights], axis=1)
            acc[h] = acc[h] * shrink + jnp.dot(weights, values, preferred_element_type=jnp.float32)

    head_units = heads // UNIT_HEADS
    units = tiles * head_units
    segments = 4

    def first_hop(c):
        await_arrival(c, 0, 1)
        start(c, 2, 3, 5, 6)

        @pl.when(c + 2 < chunks)
        def _():
            start(c + 2, 0, 1, 4)

    def second_hop(c):
        await_arrival(c, 2, 3)
        start(c, 7)

    for copy in own_hidden + weights_in + query_in:
        copy.wait()
    first_hop(0)
    second_hop(0)

    def live(c):
        return (c >= 0) & (c < chunks)

    def segment(g, carry):
        period, seg = g // segments, g % segments
        ready = period - 2

        @pl.when((seg == 0) & live(ready))
        def _():
            await_arrival(ready, 22, 23, 24, 25)

            @pl.when(ready == 0)
            def _():
                meta_await(7, 8)

        @pl.when((seg == 1) & live(period))
        def _():
            c = period
            await_arrival(c, 4, 5, 6, 7)
            project(c)
            start(c, 8, 9)

        @pl.when((seg == 1) & live(period - 1))
        def _():
            c = period - 1
            await_arrival(c, 14, 15, 16, 17)
            start(c, 18, 19, 20, 21)

            @pl.when(c == 0)
            def _():
                meta_await(3, 4)
                meta_start(5, 6)

        @pl.when((seg == 2) & live(period + 1))
        def _():
            first_hop(period + 1)

        @pl.when((seg == 2) & live(period))
        def _():
            c = period
            await_arrival(c, 8, 9)
            start(c, 10, 11, 12, 13)

            @pl.when(c == 0)
            def _():
                meta_await(0)
                meta_start(1, 2)

        @pl.when((seg == 3) & live(period - 1))
        def _():
            c = period - 1
            await_arrival(c, 18, 19, 20, 21)
            start(c, 22, 23, 24, 25)

            @pl.when(c == 0)
            def _():
                meta_await(5, 6)
                meta_start(7, 8)

        @pl.when((seg == 3) & live(period))
        def _():
            c = period
            await_arrival(c, 10, 11, 12, 13)
            start(c, 14, 15, 16, 17)

            @pl.when(c == 0)
            def _():
                meta_await(1, 2)
                meta_start(3, 4)

        @pl.when((seg == 3) & live(period + 1))
        def _():
            second_hop(period + 1)

        @pl.when(live(ready))
        def _():
            def one(u, inner):
                kt, hp = u // head_units, u % head_units

                @pl.when(kt < own_tile)
                def _():
                    attend(ready, kt, hp, False)

                @pl.when(kt == own_tile)
                def _():
                    attend(ready, kt, hp, True)

                return inner

            lax.fori_loop(seg * units // segments, (seg + 1) * units // segments, one, 0)

        @pl.when((seg == segments - 1) & live(ready))
        def _():
            @pl.when(ready == 0)
            def _():
                count_incoming()

            decode_chunk(ready)

        return carry

    lax.fori_loop(0, (chunks + 2) * segments, segment, 0)

    for h in range(heads):
        total = jnp.sum(row_sum[h], axis=1, keepdims=True)
        out[:, h * lanes : (h + 1) * lanes] = (acc[h] / total).astype(out.dtype)
    decoded = jnp.transpose(dec_acc[...] / dec_sum[...])
    for h in range(heads):
        decode_out[:, h * lanes : (h + 1) * lanes] = decoded[
            h * decode_rows : (h + 1) * decode_rows, :
        ].astype(decode_out.dtype)

    def drain(c, carry):
        for k in range(N_COPIES):
            remote(c, k).wait_send()
        return carry

    lax.fori_loop(0, chunks, drain, 0)
    for k in range(N_META):
        meta_copy(k).wait_send()


def per_device(
    prefill_hidden,
    norm_gain,
    key_weight,
    value_weight,
    prefill_query,
    resident_keys,
    resident_values,
    decode_query,
    page_owner,
    block_table,
    context_len,
):
    stretch, width = prefill_hidden.shape
    heads = prefill_query.shape[1] // HD
    pool = resident_keys.shape[0]
    features = key_weight.shape[0]
    rows = stretch // CHUNKS
    tables = [jnp.asarray(each) for each in rope_tables(stretch, 32)]
    anywhere = pl.BlockSpec(memory_space=pl.ANY)
    vmem = pl.BlockSpec(memory_space=pltpu.VMEM)
    smem = pl.BlockSpec(memory_space=pltpu.SMEM)
    f32, bf16, i32 = jnp.float32, jnp.bfloat16, jnp.int32
    return pl.pallas_call(
        kernel,
        out_shape=(
            jax.ShapeDtypeStruct(prefill_query.shape, bf16),
            jax.ShapeDtypeStruct(decode_query.shape, bf16),
        ),
        in_specs=[
            anywhere,
            vmem,
            anywhere,
            anywhere,
            anywhere,
            anywhere,
            anywhere,
            vmem,
            smem,
            smem,
            smem,
            vmem,
            vmem,
            vmem,
            vmem,
        ],
        out_specs=(vmem, vmem),
        scratch_shapes=[
            pltpu.VMEM((CHUNKS, features // width, rows, width), bf16),
            pltpu.VMEM((features, 2 * HD), bf16),
            pltpu.VMEM((CHUNKS, 2, 4, 4, rows, HD), bf16),
            pltpu.VMEM((CHUNKS, 2, 4, 4, rows, HD), bf16),
            pltpu.VMEM((2, 4, 4, stretch // PAGE, HD), i32),
            pltpu.VMEM((heads, stretch, HD), bf16),
            pltpu.VMEM((pool, PAGE, HD), bf16),
            pltpu.VMEM((pool, PAGE, HD), bf16),
            pltpu.VMEM((heads * decode_query.shape[0], HD), bf16),
            pltpu.VMEM((stretch, HD), f32),
            pltpu.VMEM((stretch, HD), f32),
            pltpu.VMEM((heads, stretch, HD), f32),
            pltpu.VMEM((heads, stretch, HD), f32),
            pltpu.VMEM((heads, stretch, HD), f32),
            pltpu.VMEM((block_table.shape[1], HD), i32),
            pltpu.VMEM((1, HD), i32),
            pltpu.VMEM((32, stretch // PAGE, HD), f32),
            pltpu.VMEM((32, stretch // PAGE, HD), f32),
            pltpu.VMEM((1, HD), f32),
            pltpu.VMEM((1, HD), f32),
            pltpu.VMEM((HD, HD), f32),
            pltpu.SemaphoreType.DMA((CHUNKS + 4 + heads,)),
            pltpu.SemaphoreType.DMA((CHUNKS, N_COPIES)),
            pltpu.SemaphoreType.DMA((CHUNKS, N_COPIES)),
            pltpu.SemaphoreType.DMA((N_META,)),
            pltpu.SemaphoreType.DMA((N_META,)),
        ],
        compiler_params=pltpu.CompilerParams(
            collective_id=0, has_side_effects=True, vmem_limit_bytes=60 * 1024 * 1024
        ),
        name="attention_layer",
    )(
        prefill_hidden,
        norm_gain.reshape(1, features),
        key_weight,
        value_weight,
        prefill_query,
        resident_keys,
        resident_values,
        decode_query,
        page_owner,
        block_table,
        context_len,
        *tables,
    )


def solution(mesh):
    return jax.shard_map(
        per_device,
        mesh=mesh,
        in_specs=(
            P("section", "tp"),
            P(),
            P(None, "tp"),
            P(None, "tp"),
            P("section", "tp"),
            P("section", None, "tp"),
            P("section", None, "tp"),
            P("section", "tp"),
            P("section"),
            P("section", None),
            P("section"),
        ),
        out_specs=(P("section", "tp"), P("section", "tp")),
        check_vma=False,
    )
```

```python
import functools
import math

import numpy as np

import jax
import jax.numpy as jnp
from jax import lax
from jax.experimental import pallas as pl
from jax.experimental.pallas import tpu as pltpu
from jax.sharding import PartitionSpec as P

MESH = pl.DeviceIdType.MESH
HD = 128
PAGE = 16
NORM_EPSILON = 1e-05
ROPE_THETA = 500000.0
NEG = -1e30
CHUNKS = 8
TILE_Y = 4
UNIT_HEADS = 4
GROUP = 2
LAG = 6
AHEAD = 2
N_COPIES = 22
N_META = 7
POW = math.log2(math.e) / math.sqrt(HD)

NT = (((1,), (1,)), ((), ()))
TN = (((0,), (0,)), ((), ()))


def rope_tables(stretch, sections):
    half = HD // 2
    exponent = np.arange(half, dtype=np.float32) * np.float32(-2.0 * math.log(ROPE_THETA) / HD)
    frequency = np.exp(exponent).astype(np.float64)
    inner = np.arange(stretch)[:, None] * frequency[None, :]
    outer = (np.arange(sections) * stretch)[:, None] * frequency[None, :]

    def both(angles):
        cosine = np.concatenate([np.cos(angles), np.cos(angles)], axis=1)
        sine = np.concatenate([np.sin(angles), np.sin(angles)], axis=1)
        return cosine.astype(np.float32), sine.astype(np.float32)

    return both(inner) + both(outer)


def kernel(
    hidden,
    gain,
    key_weight,
    value_weight,
    query,
    resident_keys,
    resident_values,
    decode_query,
    owner,
    table,
    context,
    cos_in,
    sin_in,
    cos_out,
    sin_out,
    out,
    decode_out,
    hid,
    wkv,
    kb,
    vb,
    meta,
    qs,
    rk,
    rv,
    dqm,
    cosine,
    sine,
    row_max,
    row_sum,
    acc,
    visible_pages,
    last_page,
    count_full,
    count_last,
    page_full,
    page_last,
    dec_max,
    dec_sum,
    dec_acc,
    local_sem,
    send_sem,
    recv_sem,
    meta_send,
    meta_recv,
):
    stretch = hidden.shape[0]
    width = hidden.shape[1]
    chunks = kb.shape[0]
    rows = stretch // chunks
    half_rows = rows // 2
    heads = qs.shape[0]
    pages_chunk = rows // PAGE
    pages_here = stretch // PAGE
    pool = rk.shape[0]
    max_pages = table.shape[1]
    decode_rows = decode_query.shape[0]
    lanes = 128

    s = lax.axis_index("section")
    t = lax.axis_index("tp")
    zh, core = t // 2, t % 2
    zl, y, x = s // 16, (s // 4) % 4, s % 4
    t_r, t_l, t_o = ((zh + 1) % 4) * 2 + core, ((zh + 3) % 4) * 2 + core, ((zh + 2) % 4) * 2 + core
    other = 1 - core
    t_p = zh * 2 + other
    p_r, p_l, p_o = ((zh + 1) % 4) * 2 + other, ((zh + 3) % 4) * 2 + other, ((zh + 2) % 4) * 2 + other
    xp, xm, xo = (x + 1) % 4, (x + 3) % 4, (x + 2) % 4
    yp, ym, yo = (y + 1) % 4, (y + 3) % 4, (y + 2) % 4
    zo = 1 - zl

    def at_section(zz, yy, xx):
        return (zz * 16 + yy * 4 + xx, t)

    z_right, z_left, partner = (s, t_r), (s, t_l), (s, t_p)
    z_other = at_section(zo, y, x)
    x_right, x_left = at_section(zl, y, xp), at_section(zl, y, xm)
    y_up, y_down = at_section(zl, yp, x), at_section(zl, ym, x)
    x_far, y_far = at_section(zl, y, xo), at_section(zl, yo, x)

    def routes(c):
        top, bottom = pl.ds(0, half_rows), pl.ds(half_rows, half_rows)
        mine = hidden.at[pl.ds(pl.multiple_of(c * rows, rows), rows), :]
        return (
            (mine, hid.at[c, t], hid.at[c, t_l], z_right),
            (mine, hid.at[c, t], hid.at[c, t_r], z_left),
            (hid.at[c, t_l, top], hid.at[c, t_l, top], hid.at[c, t_o, top], z_right),
            (hid.at[c, t_r, bottom], hid.at[c, t_r, bottom], hid.at[c, t_o, bottom], z_left),
            (mine, hid.at[c, t], hid.at[c, t_p], partner),
            (hid.at[c, t_l], hid.at[c, t_l], hid.at[c, p_l], partner),
            (hid.at[c, t_r], hid.at[c, t_r], hid.at[c, p_r], partner),
            (hid.at[c, t_o], hid.at[c, t_o], hid.at[c, p_o], partner),
            (kb.at[c, zl, y, x], kb.at[c, zl, y, x], kb.at[c, zo, y, x], z_other),
            (vb.at[c, zl, y, x], vb.at[c, zl, y, x], vb.at[c, zo, y, x], z_other),
            (kb.at[c, :, y, x], kb.at[c, :, y, x], kb.at[c, :, y, xm], x_right),
            (kb.at[c, :, y, x], kb.at[c, :, y, x], kb.at[c, :, y, xp], x_left),
            (kb.at[c, :, y, x], kb.at[c, :, y, x], kb.at[c, :, y, xo], x_far),
            (vb.at[c, :, y, x], vb.at[c, :, y, x], vb.at[c, :, ym, x], y_up),
            (vb.at[c, :, y, x], vb.at[c, :, y, x], vb.at[c, :, yp, x], y_down),
            (vb.at[c, :, y, x], vb.at[c, :, y, x], vb.at[c, :, yo, x], y_far),
            (kb.at[c, :, y], kb.at[c, :, y], kb.at[c, :, ym], y_up),
            (kb.at[c, :, y], kb.at[c, :, y], kb.at[c, :, yp], y_down),
            (kb.at[c, :, y], kb.at[c, :, y], kb.at[c, :, yo], y_far),
            (vb.at[c, :, :, x], vb.at[c, :, :, x], vb.at[c, :, :, xm], x_right),
            (vb.at[c, :, :, x], vb.at[c, :, :, x], vb.at[c, :, :, xp], x_left),
            (vb.at[c, :, :, x], vb.at[c, :, :, x], vb.at[c, :, :, xo], x_far),
        )

    meta_routes = (
        (meta.at[zl, y, x], meta.at[zo, y, x], z_other),
        (meta.at[:, y, x], meta.at[:, y, xm], x_right),
        (meta.at[:, y, x], meta.at[:, y, xp], x_left),
        (meta.at[:, y, x], meta.at[:, y, xo], x_far),
        (meta.at[:, y], meta.at[:, ym], y_up),
        (meta.at[:, y], meta.at[:, yp], y_down),
        (meta.at[:, y], meta.at[:, yo], y_far),
    )

    def remote(c, k):
        source, target, _, device = routes(c)[k]
        return pltpu.make_async_remote_copy(
            src_ref=source,
            dst_ref=target,
            send_sem=send_sem.at[c, k],
            recv_sem=recv_sem.at[c, k],
            device_id=device,
            device_id_type=MESH,
        )

    def arrival(c, k):
        _, _, landing, device = routes(c)[k]
        return pltpu.make_async_remote_copy(
            src_ref=landing,
            dst_ref=landing,
            send_sem=send_sem.at[c, k],
            recv_sem=recv_sem.at[c, k],
            device_id=device,
            device_id_type=MESH,
        )

    def start(c, *ks):
        for k in ks:
            remote(c, k).start()

    def await_arrival(c, *ks):
        for k in ks:
            arrival(c, k).wait_recv()

    def meta_copy(k):
        source, _, device = meta_routes[k]
        return pltpu.make_async_remote_copy(
            src_ref=source,
            dst_ref=source,
            send_sem=meta_send.at[k],
            recv_sem=meta_recv.at[k],
            device_id=device,
            device_id_type=MESH,
        )

    def meta_arrival(k):
        _, landing, device = meta_routes[k]
        return pltpu.make_async_remote_copy(
            src_ref=landing,
            dst_ref=landing,
            send_sem=meta_send.at[k],
            recv_sem=meta_recv.at[k],
            device_id=device,
            device_id_type=MESH,
        )

    def meta_start(*ks):
        for k in ks:
            meta_copy(k).start()

    def meta_await(*ks):
        for k in ks:
            meta_arrival(k).wait_recv()

    own_hidden = [
        pltpu.make_async_copy(
            hidden.at[pl.ds(c * rows, rows), :], hid.at[c, t], local_sem.at[c]
        )
        for c in range(chunks)
    ]
    weights_in = [
        pltpu.make_async_copy(key_weight, wkv.at[:, pl.ds(0, lanes)], local_sem.at[chunks]),
        pltpu.make_async_copy(value_weight, wkv.at[:, pl.ds(lanes, lanes)], local_sem.at[chunks + 1]),
    ]
    resident_in = [
        pltpu.make_async_copy(resident_keys, rk, local_sem.at[chunks + 2]),
        pltpu.make_async_copy(resident_values, rv, local_sem.at[chunks + 3]),
    ]
    query_in = [
        pltpu.make_async_copy(
            query.at[:, pl.ds(h * lanes, lanes)], qs.at[h], local_sem.at[chunks + 4 + h]
        )
        for h in range(heads)
    ]

    neighbours = (
        z_right,
        z_left,
        partner,
        z_other,
        x_right,
        x_left,
        x_far,
        y_up,
        y_down,
        y_far,
    )
    barrier = pltpu.get_barrier_semaphore()
    for device in neighbours:
        pl.semaphore_signal(barrier, inc=1, device_id=device, device_id_type=MESH)
    pl.semaphore_wait(barrier, len(neighbours))
    for c in range(AHEAD):
        start(c, 0, 1, 4)
    for copy in own_hidden + resident_in + weights_in + query_in:
        copy.start()

    owners = [owner[i] for i in range(pages_here)]
    page_row = lax.broadcasted_iota(jnp.int32, (pages_here, lanes), 0)
    codes = jnp.zeros((pages_here, lanes), jnp.int32)
    for i in range(pages_here):
        rank = jnp.int32(0)
        for j in range(i):
            rank = rank + jnp.where(owners[j] == owners[i], 1, 0).astype(jnp.int32)
        code = owners[i] * (count_full.shape[0] - pool) + s * 2 + rank
        codes = jnp.where(page_row == i, code, codes)
    meta[zl, y, x] = codes

    lane_row = lax.broadcasted_iota(jnp.int32, (1, lanes), 1) % decode_rows
    lengths = jnp.zeros((1, lanes), jnp.int32)
    for r in range(decode_rows):
        lengths = jnp.where(lane_row == r, context[r], lengths)
    full_pages = lax.shift_right_logical(lengths - 1, 4)
    last_tokens = lengths - full_pages * PAGE
    last_page[...] = jnp.zeros((1, lanes), jnp.int32)

    def table_row(j, carry):
        entries = jnp.zeros((1, lanes), jnp.int32)
        for r in range(decode_rows):
            entries = jnp.where(lane_row == r, table[r, j], entries)
        visible_pages[pl.ds(j, 1), :] = jnp.where(full_pages > j, entries, -1)
        last_page[...] = jnp.where(full_pages == j, entries, last_page[...])
        return carry

    lax.fori_loop(0, max_pages, table_row, 0)
    meta_start(0)

    for h in range(heads):
        dqm[h * decode_rows : (h + 1) * decode_rows, :] = decode_query[:, h * lanes : (h + 1) * lanes]
    ca, sa = cos_out[pl.ds(s, 1), :], sin_out[pl.ds(s, 1), :]
    low = lax.broadcasted_iota(jnp.int32, (1, lanes), 1) < lanes // 2
    cosine[...] = ca * cos_in[...] - sa * sin_in[...]
    sine[...] = jnp.where(low, -1.0, 1.0) * (sa * cos_in[...] + ca * sin_in[...])
    row_max[...] = jnp.full(row_max.shape, NEG, jnp.float32)
    row_sum[...] = jnp.zeros(row_sum.shape, jnp.float32)
    acc[...] = jnp.zeros(acc.shape, jnp.float32)
    dec_max[...] = jnp.full(dec_max.shape, NEG, jnp.float32)
    dec_sum[...] = jnp.zeros(dec_sum.shape, jnp.float32)
    dec_acc[...] = jnp.zeros(dec_acc.shape, jnp.float32)

    tile_pages = 32

    def count_pages(i, carry):
        first = pl.multiple_of(i * tile_pages, tile_pages)
        ids = first + lax.broadcasted_iota(jnp.int32, (tile_pages, lanes), 0)

        def step(j, total):
            return total + jnp.where(ids == visible_pages[pl.ds(j, 1), :], 1.0, 0.0)

        count_full[pl.ds(first, tile_pages), :] = lax.fori_loop(
            0, max_pages, step, jnp.zeros(ids.shape, jnp.float32), unroll=8
        )
        count_last[pl.ds(first, tile_pages), :] = jnp.where(ids == last_page[...], 1.0, 0.0)
        return carry

    lax.fori_loop(0, count_full.shape[0] // tile_pages, count_pages, 0)
    slots = count_full.shape[0] - pool

    def decode_tile(keys, values, counts):
        scores = lax.dot_general(keys, dqm[...], NT, preferred_element_type=jnp.float32)
        scores = jnp.where(counts > 0.0, scores, NEG)
        old = dec_max[...]
        new = jnp.maximum(old, jnp.max(scores, axis=0, keepdims=True))
        weights = counts * jnp.exp2((scores - new) * POW)
        shrink = jnp.exp2((old - new) * POW)
        dec_max[...] = new
        dec_sum[...] = dec_sum[...] * shrink + jnp.sum(weights, axis=0, keepdims=True)
        dec_acc[...] = dec_acc[...] * shrink + lax.dot_general(
            values, weights.astype(jnp.bfloat16), TN, preferred_element_type=jnp.float32
        )

    token_of = lax.broadcasted_iota(jnp.int32, (PAGE, lanes), 0)
    in_last = jnp.where(token_of < last_tokens, 1.0, 0.0)

    def token_counts(full, last):
        return jnp.broadcast_to(full, (PAGE, lanes)) + in_last * jnp.broadcast_to(
            last, (PAGE, lanes)
        )

    def resident_tile(i):
        first = pl.multiple_of(i * tile_pages, tile_pages)
        full = count_full[pl.ds(first, tile_pages), :]
        last = count_last[pl.ds(first, tile_pages), :]
        counts = [token_counts(full[p : p + 1], last[p : p + 1]) for p in range(tile_pages)]
        decode_tile(
            rk[pl.ds(first, tile_pages)].reshape(tile_pages * PAGE, lanes),
            rv[pl.ds(first, tile_pages)].reshape(tile_pages * PAGE, lanes),
            jnp.concatenate(counts, axis=0),
        )

    def count_incoming():
        slot = lax.broadcasted_iota(jnp.int32, (pages_here, lanes), 1)
        picks = []
        for i in range(32):
            code = meta[i // 16, i // 4 % 4, i % 4] - s * slots
            picks.append(jnp.where(code == slot, 1.0, 0.0).astype(jnp.bfloat16))
        table_of = jnp.concatenate([count_full[pool:, :], count_last[pool:, :]], axis=1)
        table_of = table_of.astype(jnp.bfloat16)
        counts = jnp.dot(
            jnp.concatenate(picks, axis=0)[:, :slots], table_of, preferred_element_type=jnp.float32
        )
        page_full[...] = counts[:, :lanes]
        page_last[...] = counts[:, lanes:]

    def decode_chunk(c):
        counts = []
        for i in range(32):
            for p in range(pages_chunk):
                at = pl.ds(i * pages_here + c * pages_chunk + p, 1)
                counts.append(token_counts(page_full[at, :], page_last[at, :]))
        decode_tile(
            kb[c].reshape(32 * rows, lanes),
            vb[c].reshape(32 * rows, lanes),
            jnp.concatenate(counts, axis=0),
        )

    shards = hid.shape[1]

    def project(c):
        squares = jnp.zeros((rows, 1), jnp.float32)
        for j in range(shards):
            block = hid[c, j].astype(jnp.float32)
            squares = squares + jnp.sum(block * block, axis=1, keepdims=True)
        inverse = lax.rsqrt(squares * (1.0 / (shards * width)) + NORM_EPSILON)
        total = jnp.zeros((rows, 2 * lanes), jnp.float32)
        for j in range(shards):
            block = hid[c, j].astype(jnp.float32)
            normed = (block * inverse * gain[:, j * width : (j + 1) * width]).astype(jnp.bfloat16)
            total = total + jnp.dot(
                normed, wkv[j * width : (j + 1) * width, :], preferred_element_type=jnp.float32
            )
        keys = total[:, :lanes]
        at = pl.ds(pl.multiple_of(c * rows, rows), rows)
        keys = keys * cosine[at, :] + pltpu.roll(keys, lanes // 2, 1) * sine[at, :]
        kb[c, zl, y, x] = keys.astype(jnp.bfloat16)
        vb[c, zl, y, x] = total[:, lanes:].astype(jnp.bfloat16)

    tile_sections = 4 * TILE_Y
    tile_keys = GROUP * tile_sections * rows
    tiles = 32 // tile_sections
    own_tile = s // tile_sections

    def attend(c, kt, hp, masked):
        first_y = kt * TILE_Y
        at = (pl.ds(c, GROUP), first_y // 4, pl.ds(first_y % 4, TILE_Y))
        keys = kb[at].reshape(tile_keys, lanes)
        values = vb[at].reshape(tile_keys, lanes)
        if masked:
            n = lax.broadcasted_iota(jnp.int32, (stretch, lanes), 1)
            query_pos = s * stretch + lax.broadcasted_iota(jnp.int32, (stretch, lanes), 0)
        def score(i):
            return lax.dot_general(
                qs[hp * UNIT_HEADS + i], keys, NT, preferred_element_type=jnp.float32
            )

        following = score(0)
        for i in range(UNIT_HEADS):
            h = hp * UNIT_HEADS + i
            scores = following
            if i + 1 < UNIT_HEADS:
                following = score(i + 1)
            pieces = [scores[:, j * lanes : (j + 1) * lanes] for j in range(tile_keys // lanes)]
            if masked:
                for j in range(len(pieces)):
                    at = j * lanes + n
                    part, rest = at // (tile_sections * rows), at % (tile_sections * rows)
                    key_pos = (kt * tile_sections + rest // rows) * stretch
                    key_pos = key_pos + (c + part) * rows + rest % rows
                    pieces[j] = jnp.where(key_pos <= query_pos, pieces[j], NEG)
            top = functools.reduce(jnp.maximum, pieces)
            old = row_max[h]
            new = jnp.maximum(old, jnp.max(top, axis=1, keepdims=True))
            shrink = jnp.exp2((old - new) * POW)
            weights = [jnp.exp2((piece - new) * POW) for piece in pieces]
            row_max[h] = new
            row_sum[h] = row_sum[h] * shrink + functools.reduce(jnp.add, weights)
            weights = jnp.concatenate([w.astype(jnp.bfloat16) for w in weights], axis=1)
            acc[h] = acc[h] * shrink + jnp.dot(weights, values, preferred_element_type=jnp.float32)

    head_units = heads // UNIT_HEADS
    units = tiles * head_units
    segments = 4

    def live(c):
        return (c >= 0) & (c < chunks)

    def first_hop(c):
        await_arrival(c, 0, 1)
        start(c, 2, 3, 5, 6)

        @pl.when(c + AHEAD < chunks)
        def _():
            start(c + AHEAD, 0, 1, 4)

    def second_hop(c):
        await_arrival(c, 2, 3)
        start(c, 7)

    def project_and_pair(c):
        await_arrival(c, 4, 5, 6, 7)
        project(c)
        start(c, 8, 9)

    def first_stage(c):
        await_arrival(c, 8, 9)
        start(c, 10, 11, 12, 13, 14, 15)

        @pl.when(c == 0)
        def _():
            meta_await(0)
            meta_start(1, 2, 3)

    def second_stage(c):
        await_arrival(c, 10, 11, 12, 13, 14, 15)
        start(c, 16, 17, 18, 19, 20, 21)

        @pl.when(c == 0)
        def _():
            meta_await(1, 2, 3)
            meta_start(4, 5, 6)

    def gathered(c):
        await_arrival(c, 16, 17, 18, 19, 20, 21)

        @pl.when(c == 0)
        def _():
            meta_await(4, 5, 6)
            count_incoming()

    plan = (
        (0, 2, project_and_pair),
        (0, LAG, gathered),
        (0, 0, first_hop),
        (0, 3, first_stage),
        (2, 1, second_hop),
        (2, 4, second_stage),
    )

    for copy in own_hidden + weights_in + query_in + resident_in:
        copy.wait()

    def segment(g, carry):
        period, seg = g // segments, g % segments
        ready = period - LAG

        for at, lag, handler in plan:

            @pl.when((seg == at) & live(period - lag))
            def _(handler=handler, lag=lag):
                handler(period - lag)

        @pl.when(g < pool // tile_pages)
        def _():
            resident_tile(g)

        beat = ready - (GROUP - 1)

        @pl.when((beat >= 0) & (beat < chunks))
        def _():
            group = beat // GROUP * GROUP
            stage = beat % GROUP * segments + seg
            stages = GROUP * segments

            def one(u, inner):
                kt, hp = u // head_units, u % head_units

                @pl.when(kt < own_tile)
                def _():
                    attend(group, kt, hp, False)

                @pl.when(kt == own_tile)
                def _():
                    attend(group, kt, hp, True)

                return inner

            lax.fori_loop(stage * units // stages, (stage + 1) * units // stages, one, 0)

        @pl.when((seg == segments - 1) & live(ready))
        def _():
            decode_chunk(ready)

        return carry

    lax.fori_loop(0, (chunks + LAG + GROUP - 1) * segments, segment, 0)

    for h in range(heads):
        total = jnp.sum(row_sum[h], axis=1, keepdims=True)
        out[:, h * lanes : (h + 1) * lanes] = (acc[h] / total).astype(out.dtype)
    decoded = jnp.transpose(dec_acc[...] / dec_sum[...])
    for h in range(heads):
        decode_out[:, h * lanes : (h + 1) * lanes] = decoded[
            h * decode_rows : (h + 1) * decode_rows, :
        ].astype(decode_out.dtype)

    def drain(c, carry):
        for k in range(N_COPIES):
            remote(c, k).wait_send()
        return carry

    lax.fori_loop(0, chunks, drain, 0)
    for k in range(N_META):
        meta_copy(k).wait_send()


def per_device(
    prefill_hidden,
    norm_gain,
    key_weight,
    value_weight,
    prefill_query,
    resident_keys,
    resident_values,
    decode_query,
    page_owner,
    block_table,
    context_len,
):
    stretch, width = prefill_hidden.shape
    heads = prefill_query.shape[1] // HD
    pool = resident_keys.shape[0]
    features = key_weight.shape[0]
    rows = stretch // CHUNKS
    tables = [jnp.asarray(each) for each in rope_tables(stretch, 32)]
    anywhere = pl.BlockSpec(memory_space=pl.ANY)
    vmem = pl.BlockSpec(memory_space=pltpu.VMEM)
    smem = pl.BlockSpec(memory_space=pltpu.SMEM)
    f32, bf16, i32 = jnp.float32, jnp.bfloat16, jnp.int32
    return pl.pallas_call(
        kernel,
        out_shape=(
            jax.ShapeDtypeStruct(prefill_query.shape, bf16),
            jax.ShapeDtypeStruct(decode_query.shape, bf16),
        ),
        in_specs=[
            anywhere,
            vmem,
            anywhere,
            anywhere,
            anywhere,
            anywhere,
            anywhere,
            vmem,
            smem,
            smem,
            smem,
            vmem,
            vmem,
            vmem,
            vmem,
        ],
        out_specs=(vmem, vmem),
        scratch_shapes=[
            pltpu.VMEM((CHUNKS, features // width, rows, width), bf16),
            pltpu.VMEM((features, 2 * HD), bf16),
            pltpu.VMEM((CHUNKS, 2, 4, 4, rows, HD), bf16),
            pltpu.VMEM((CHUNKS, 2, 4, 4, rows, HD), bf16),
            pltpu.VMEM((2, 4, 4, stretch // PAGE, HD), i32),
            pltpu.VMEM((heads, stretch, HD), bf16),
            pltpu.VMEM((pool, PAGE, HD), bf16),
            pltpu.VMEM((pool, PAGE, HD), bf16),
            pltpu.VMEM((heads * decode_query.shape[0], HD), bf16),
            pltpu.VMEM((stretch, HD), f32),
            pltpu.VMEM((stretch, HD), f32),
            pltpu.VMEM((heads, stretch, HD), f32),
            pltpu.VMEM((heads, stretch, HD), f32),
            pltpu.VMEM((heads, stretch, HD), f32),
            pltpu.VMEM((block_table.shape[1], HD), i32),
            pltpu.VMEM((1, HD), i32),
            pltpu.VMEM((pool + 64, HD), f32),
            pltpu.VMEM((pool + 64, HD), f32),
            pltpu.VMEM((32 * stretch // PAGE, HD), f32),
            pltpu.VMEM((32 * stretch // PAGE, HD), f32),
            pltpu.VMEM((1, HD), f32),
            pltpu.VMEM((1, HD), f32),
            pltpu.VMEM((HD, HD), f32),
            pltpu.SemaphoreType.DMA((CHUNKS + 4 + heads,)),
            pltpu.SemaphoreType.DMA((CHUNKS, N_COPIES)),
            pltpu.SemaphoreType.DMA((CHUNKS, N_COPIES)),
            pltpu.SemaphoreType.DMA((N_META,)),
            pltpu.SemaphoreType.DMA((N_META,)),
        ],
        compiler_params=pltpu.CompilerParams(
            collective_id=0, has_side_effects=True, vmem_limit_bytes=60 * 1024 * 1024
        ),
        name="attention_layer",
    )(
        prefill_hidden,
        norm_gain.reshape(1, features),
        key_weight,
        value_weight,
        prefill_query,
        resident_keys,
        resident_values,
        decode_query,
        page_owner,
        block_table,
        context_len,
        *tables,
    )


def solution(mesh):
    return jax.shard_map(
        per_device,
        mesh=mesh,
        in_specs=(
            P("section", "tp"),
            P(),
            P(None, "tp"),
            P(None, "tp"),
            P("section", "tp"),
            P("section", None, "tp"),
            P("section", None, "tp"),
            P("section", "tp"),
            P("section"),
            P("section", None),
            P("section"),
        ),
        out_specs=(P("section", "tp"), P("section", "tp")),
        check_vma=False,
    )
```

```python
import functools
import math

import numpy as np

import jax
import jax.numpy as jnp
from jax import lax
from jax.experimental import pallas as pl
from jax.experimental.pallas import tpu as pltpu
from jax.sharding import PartitionSpec as P

MESH = pl.DeviceIdType.MESH
HD = 128
PAGE = 16
NORM_EPSILON = 1e-05
ROPE_THETA = 500000.0
NEG = -1e30
CHUNKS = 8
TILE_Y = 4
UNIT_HEADS = 8
GROUP = 2
LAG = 6
AHEAD = 2
GROUPS = ((0, 1), (2, 3), (4, 5, 6, 7), (8, 9), (10, 11, 12, 13, 14, 15), (16, 17, 18, 19, 20, 21))
GROUP_OF = tuple(g for g, ks in enumerate(GROUPS) for _ in ks)
N_META = 7
POW = math.log2(math.e) / math.sqrt(HD)

NT = (((1,), (1,)), ((), ()))
TN = (((0,), (0,)), ((), ()))


def rope_tables(stretch, sections):
    half = HD // 2
    exponent = np.arange(half, dtype=np.float32) * np.float32(-2.0 * math.log(ROPE_THETA) / HD)
    frequency = np.exp(exponent).astype(np.float64)
    inner = np.arange(stretch)[:, None] * frequency[None, :]
    outer = (np.arange(sections) * stretch)[:, None] * frequency[None, :]

    def both(angles):
        cosine = np.concatenate([np.cos(angles), np.cos(angles)], axis=1)
        sine = np.concatenate([np.sin(angles), np.sin(angles)], axis=1)
        return cosine.astype(np.float32), sine.astype(np.float32)

    return both(inner) + both(outer)


def kernel(
    hidden,
    gain,
    key_weight,
    value_weight,
    query,
    resident_keys,
    resident_values,
    decode_query,
    owner,
    table,
    context,
    cos_in,
    sin_in,
    cos_out,
    sin_out,
    out,
    decode_out,
    hid,
    wkv,
    kb,
    vb,
    meta,
    qs,
    rk,
    rv,
    dqm,
    cosine,
    sine,
    row_max,
    row_sum,
    acc,
    visible_pages,
    last_page,
    count_full,
    count_last,
    slot_page,
    slot_index,
    dec_max,
    dec_sum,
    dec_acc,
    local_sem,
    send_sem,
    recv_sem,
    meta_send,
    meta_recv,
):
    stretch = hidden.shape[0]
    width = hidden.shape[1]
    chunks = kb.shape[0]
    rows = stretch // chunks
    half_rows = rows // 2
    heads = qs.shape[0]
    pages_chunk = rows // PAGE
    pages_here = stretch // PAGE
    pool = rk.shape[0]
    max_pages = table.shape[1]
    decode_rows = decode_query.shape[0]
    lanes = 128

    s = lax.axis_index("section")
    t = lax.axis_index("tp")
    zh, core = t // 2, t % 2
    zl, y, x = s // 16, (s // 4) % 4, s % 4
    t_r, t_l, t_o = ((zh + 1) % 4) * 2 + core, ((zh + 3) % 4) * 2 + core, ((zh + 2) % 4) * 2 + core
    other = 1 - core
    t_p = zh * 2 + other
    xp, xm, xo = (x + 1) % 4, (x + 3) % 4, (x + 2) % 4
    yp, ym, yo = (y + 1) % 4, (y + 3) % 4, (y + 2) % 4
    zo = 1 - zl

    def at_section(zz, yy, xx):
        return (zz * 16 + yy * 4 + xx, t)

    z_right, z_left, partner = (s, t_r), (s, t_l), (s, t_p)
    z_other = at_section(zo, y, x)
    x_right, x_left = at_section(zl, y, xp), at_section(zl, y, xm)
    y_up, y_down = at_section(zl, yp, x), at_section(zl, ym, x)
    x_far, y_far = at_section(zl, y, xo), at_section(zl, yo, x)

    def routes(c):
        top, bottom = pl.ds(0, half_rows), pl.ds(half_rows, half_rows)
        mine = hidden.at[pl.ds(pl.multiple_of(c * rows, rows), rows), :]
        return (
            (mine, hid.at[c, t], z_right),
            (mine, hid.at[c, t], z_left),
            (hid.at[c, t_l, top], hid.at[c, t_l, top], z_right),
            (hid.at[c, t_r, bottom], hid.at[c, t_r, bottom], z_left),
            (mine, hid.at[c, t], partner),
            (hid.at[c, t_l], hid.at[c, t_l], partner),
            (hid.at[c, t_r], hid.at[c, t_r], partner),
            (hid.at[c, t_o], hid.at[c, t_o], partner),
            (kb.at[c, zl, y, x], kb.at[c, zl, y, x], z_other),
            (vb.at[c, zl, y, x], vb.at[c, zl, y, x], z_other),
            (kb.at[c, :, y, x], kb.at[c, :, y, x], x_right),
            (kb.at[c, :, y, x], kb.at[c, :, y, x], x_left),
            (kb.at[c, :, y, x], kb.at[c, :, y, x], x_far),
            (vb.at[c, :, y, x], vb.at[c, :, y, x], y_up),
            (vb.at[c, :, y, x], vb.at[c, :, y, x], y_down),
            (vb.at[c, :, y, x], vb.at[c, :, y, x], y_far),
            (kb.at[c, :, y], kb.at[c, :, y], y_up),
            (kb.at[c, :, y], kb.at[c, :, y], y_down),
            (kb.at[c, :, y], kb.at[c, :, y], y_far),
            (vb.at[c, :, :, x], vb.at[c, :, :, x], x_right),
            (vb.at[c, :, :, x], vb.at[c, :, :, x], x_left),
            (vb.at[c, :, :, x], vb.at[c, :, :, x], x_far),
        )

    meta_routes = (
        (meta.at[zl, y, x], meta.at[zo, y, x], z_other),
        (meta.at[:, y, x], meta.at[:, y, xm], x_right),
        (meta.at[:, y, x], meta.at[:, y, xp], x_left),
        (meta.at[:, y, x], meta.at[:, y, xo], x_far),
        (meta.at[:, y], meta.at[:, ym], y_up),
        (meta.at[:, y], meta.at[:, yp], y_down),
        (meta.at[:, y], meta.at[:, yo], y_far),
    )

    def remote(c, k):
        source, target, device = routes(c)[k]
        return pltpu.make_async_remote_copy(
            src_ref=source,
            dst_ref=target,
            send_sem=send_sem.at[c, GROUP_OF[k]],
            recv_sem=recv_sem.at[c, GROUP_OF[k]],
            device_id=device,
            device_id_type=MESH,
        )

    def whole(c, g):
        view = (
            hid.at[c, pl.ds(0, 2)],
            hid.at[c, 0],
            hid.at[c, pl.ds(0, 4)],
            kb.at[c, 0, 0, pl.ds(0, 2)],
            kb.at[c, 0, pl.ds(0, 3)],
            hid.at[c, pl.ds(0, 6)],
        )[g]
        return pltpu.make_async_remote_copy(
            src_ref=view,
            dst_ref=view,
            send_sem=send_sem.at[c, g],
            recv_sem=recv_sem.at[c, g],
            device_id=partner,
            device_id_type=MESH,
        )

    def start(c, *ks):
        for k in ks:
            remote(c, k).start()

    def await_arrival(c, *ks):
        g = GROUP_OF[ks[0]]
        assert GROUPS[g] == ks
        whole(c, g).wait_recv()

    def meta_copy(k):
        source, _, device = meta_routes[k]
        return pltpu.make_async_remote_copy(
            src_ref=source,
            dst_ref=source,
            send_sem=meta_send.at[k],
            recv_sem=meta_recv.at[k],
            device_id=device,
            device_id_type=MESH,
        )

    def meta_arrival(k):
        _, landing, device = meta_routes[k]
        return pltpu.make_async_remote_copy(
            src_ref=landing,
            dst_ref=landing,
            send_sem=meta_send.at[k],
            recv_sem=meta_recv.at[k],
            device_id=device,
            device_id_type=MESH,
        )

    def meta_start(*ks):
        for k in ks:
            meta_copy(k).start()

    def meta_await(*ks):
        for k in ks:
            meta_arrival(k).wait_recv()

    own_hidden = [
        pltpu.make_async_copy(
            hidden.at[pl.ds(c * rows, rows), :], hid.at[c, t], local_sem.at[c]
        )
        for c in range(chunks)
    ]
    weights_in = [
        pltpu.make_async_copy(key_weight, wkv.at[:, pl.ds(0, lanes)], local_sem.at[chunks]),
        pltpu.make_async_copy(value_weight, wkv.at[:, pl.ds(lanes, lanes)], local_sem.at[chunks + 1]),
    ]
    resident_in = [
        pltpu.make_async_copy(resident_keys, rk, local_sem.at[chunks + 2]),
        pltpu.make_async_copy(resident_values, rv, local_sem.at[chunks + 3]),
    ]
    query_in = [
        pltpu.make_async_copy(
            query.at[:, pl.ds(h * lanes, lanes)], qs.at[h], local_sem.at[chunks + 4 + h]
        )
        for h in range(heads)
    ]

    neighbours = (
        z_right,
        z_left,
        partner,
        z_other,
        x_right,
        x_left,
        x_far,
        y_up,
        y_down,
        y_far,
    )
    barrier = pltpu.get_barrier_semaphore()
    for device in neighbours:
        pl.semaphore_signal(barrier, inc=1, device_id=device, device_id_type=MESH)
    pl.semaphore_wait(barrier, len(neighbours))
    for c in range(AHEAD):
        start(c, 0, 1, 4)
    for copy in own_hidden + resident_in + weights_in + query_in:
        copy.start()

    owners = [owner[i] for i in range(pages_here)]
    page_row = lax.broadcasted_iota(jnp.int32, (pages_here, lanes), 0)
    codes = jnp.zeros((pages_here, lanes), jnp.int32)
    for i in range(pages_here):
        rank = jnp.int32(0)
        for j in range(i):
            rank = rank + jnp.where(owners[j] == owners[i], 1, 0).astype(jnp.int32)
        code = owners[i] * (count_full.shape[0] - pool) + s * 2 + rank
        codes = jnp.where(page_row == i, code, codes)
    meta[zl, y, x] = codes

    lane_row = lax.broadcasted_iota(jnp.int32, (1, lanes), 1) % decode_rows
    lengths = jnp.zeros((1, lanes), jnp.int32)
    for r in range(decode_rows):
        lengths = jnp.where(lane_row == r, context[r], lengths)
    full_pages = lax.shift_right_logical(lengths - 1, 4)
    last_tokens = lengths - full_pages * PAGE
    last_page[...] = jnp.zeros((1, lanes), jnp.int32)

    def table_row(j, carry):
        entries = jnp.zeros((1, lanes), jnp.int32)
        for r in range(decode_rows):
            entries = jnp.where(lane_row == r, table[r, j], entries)
        visible_pages[pl.ds(j, 1), :] = jnp.where(full_pages > j, entries, -1)
        last_page[...] = jnp.where(full_pages == j, entries, last_page[...])
        return carry

    lax.fori_loop(0, max_pages, table_row, 0)
    meta_start(0)

    for h in range(heads):
        dqm[h * decode_rows : (h + 1) * decode_rows, :] = decode_query[:, h * lanes : (h + 1) * lanes]
    ca, sa = cos_out[pl.ds(s, 1), :], sin_out[pl.ds(s, 1), :]
    low = lax.broadcasted_iota(jnp.int32, (1, lanes), 1) < lanes // 2
    cosine[...] = ca * cos_in[...] - sa * sin_in[...]
    sine[...] = jnp.where(low, -1.0, 1.0) * (sa * cos_in[...] + ca * sin_in[...])
    row_max[...] = jnp.full(row_max.shape, NEG, jnp.float32)
    row_sum[...] = jnp.zeros(row_sum.shape, jnp.float32)
    acc[...] = jnp.zeros(acc.shape, jnp.float32)
    dec_max[...] = jnp.full(dec_max.shape, NEG, jnp.float32)
    dec_sum[...] = jnp.zeros(dec_sum.shape, jnp.float32)
    dec_acc[...] = jnp.zeros(dec_acc.shape, jnp.float32)

    tile_pages = 32

    def count_pages(i, carry):
        first = pl.multiple_of(i * tile_pages, tile_pages)
        ids = first + lax.broadcasted_iota(jnp.int32, (tile_pages, lanes), 0)

        def step(j, total):
            return total + jnp.where(ids == visible_pages[pl.ds(j, 1), :], 1.0, 0.0)

        count_full[pl.ds(first, tile_pages), :] = lax.fori_loop(
            0, max_pages, step, jnp.zeros(ids.shape, jnp.float32), unroll=8
        )
        count_last[pl.ds(first, tile_pages), :] = jnp.where(ids == last_page[...], 1.0, 0.0)
        return carry

    slots = count_full.shape[0] - pool

    def decode_tile(keys, values, counts):
        scores = lax.dot_general(keys, dqm[...], NT, preferred_element_type=jnp.float32)
        scores = jnp.where(counts > 0.0, scores, NEG)
        old = dec_max[...]
        new = jnp.maximum(old, jnp.max(scores, axis=0, keepdims=True))
        weights = counts * jnp.exp2((scores - new) * POW)
        shrink = jnp.exp2((old - new) * POW)
        dec_max[...] = new
        dec_sum[...] = dec_sum[...] * shrink + jnp.sum(weights, axis=0, keepdims=True)
        dec_acc[...] = dec_acc[...] * shrink + lax.dot_general(
            values, weights.astype(jnp.bfloat16), TN, preferred_element_type=jnp.float32
        )

    token_of = lax.broadcasted_iota(jnp.int32, (PAGE, lanes), 0)
    in_last = jnp.where(token_of < last_tokens, 1.0, 0.0)

    def token_counts(full, last):
        return jnp.broadcast_to(full, (PAGE, lanes)) + in_last * jnp.broadcast_to(
            last, (PAGE, lanes)
        )

    def resident_tile(i):
        first = pl.multiple_of(i * tile_pages, tile_pages)
        full = count_full[pl.ds(first, tile_pages), :]
        last = count_last[pl.ds(first, tile_pages), :]
        counts = [token_counts(full[p : p + 1], last[p : p + 1]) for p in range(tile_pages)]
        decode_tile(
            rk[pl.ds(first, tile_pages)].reshape(tile_pages * PAGE, lanes),
            rv[pl.ds(first, tile_pages)].reshape(tile_pages * PAGE, lanes),
            jnp.concatenate(counts, axis=0),
        )

    page_copy = pltpu.make_async_copy(slot_page, slot_index, local_sem.at[chunks + 4 + heads])

    def find_pages():
        lane = lax.broadcasted_iota(jnp.int32, (pages_here, lanes), 1)
        found = jnp.zeros((pages_here, lanes), jnp.int32)
        for i in range(32):
            here = (meta[i // 16, i // 4 % 4, i % 4] == s * slots + lane) & (lane // 2 == i)
            found = found + jnp.where(here, page_row, 0)
        page = jnp.minimum(jnp.sum(found, axis=0, keepdims=True), pages_here - 1)
        slot_page[0:1, :] = page // pages_chunk
        slot_page[1:2, :] = page % pages_chunk

    def decode_incoming():
        page_copy.wait()

        def fetch(k, carry):
            sec = k // 2
            chunk, page = slot_index[0, k], slot_index[1, k]
            keys = kb[chunk, sec // 16, sec // 4 % 4, sec % 4]
            values = vb[chunk, sec // 16, sec // 4 % 4, sec % 4]
            first, second = keys[:PAGE], values[:PAGE]
            for p in range(1, pages_chunk):
                part = slice(p * PAGE, (p + 1) * PAGE)
                first = jnp.where(page == p, keys[part], first)
                second = jnp.where(page == p, values[part], second)
            rk[k] = first
            rv[k] = second
            return carry

        lax.fori_loop(0, slots, fetch, 0, unroll=4)
        full, last = count_full[pool:, :], count_last[pool:, :]
        counts = [token_counts(full[p : p + 1], last[p : p + 1]) for p in range(slots)]
        decode_tile(
            rk[:slots].reshape(slots * PAGE, lanes),
            rv[:slots].reshape(slots * PAGE, lanes),
            jnp.concatenate(counts, axis=0),
        )

    shards = hid.shape[1]

    def project(c):
        squares = jnp.zeros((rows, 1), jnp.float32)
        for j in range(shards):
            block = hid[c, j].astype(jnp.float32)
            squares = squares + jnp.sum(block * block, axis=1, keepdims=True)
        inverse = lax.rsqrt(squares * (1.0 / (shards * width)) + NORM_EPSILON)
        total = jnp.zeros((rows, 2 * lanes), jnp.float32)
        for j in range(shards):
            block = hid[c, j].astype(jnp.float32)
            normed = (block * inverse * gain[:, j * width : (j + 1) * width]).astype(jnp.bfloat16)
            total = total + jnp.dot(
                normed, wkv[j * width : (j + 1) * width, :], preferred_element_type=jnp.float32
            )
        keys = total[:, :lanes]
        at = pl.ds(pl.multiple_of(c * rows, rows), rows)
        keys = keys * cosine[at, :] + pltpu.roll(keys, lanes // 2, 1) * sine[at, :]
        kb[c, zl, y, x] = keys.astype(jnp.bfloat16)
        vb[c, zl, y, x] = total[:, lanes:].astype(jnp.bfloat16)

    tile_sections = 4 * TILE_Y
    tile_keys = GROUP * tile_sections * rows
    tiles = 32 // tile_sections
    own_tile = s // tile_sections

    def attend(c, kt, hp, masked):
        first_y = kt * TILE_Y
        at = (pl.ds(c, GROUP), first_y // 4, pl.ds(first_y % 4, TILE_Y))
        keys = kb[at].reshape(tile_keys, lanes)
        values = vb[at].reshape(tile_keys, lanes)
        if masked:
            n = lax.broadcasted_iota(jnp.int32, (1, lanes), 1)
            query_pos = s * stretch + lax.broadcasted_iota(jnp.int32, (stretch, lanes), 0)
        def score(i):
            return lax.dot_general(
                qs[hp * UNIT_HEADS + i], keys, NT, preferred_element_type=jnp.float32
            )

        following = score(0)
        for i in range(UNIT_HEADS):
            h = hp * UNIT_HEADS + i
            scores = following
            if i + 1 < UNIT_HEADS:
                following = score(i + 1)
            pieces = [scores[:, j * lanes : (j + 1) * lanes] for j in range(tile_keys // lanes)]
            if masked:
                for j in range(len(pieces)):
                    at = j * lanes + n
                    part, rest = at // (tile_sections * rows), at % (tile_sections * rows)
                    key_pos = (kt * tile_sections + rest // rows) * stretch
                    key_pos = key_pos + (c + part) * rows + rest % rows
                    pieces[j] = jnp.where(key_pos <= query_pos, pieces[j], NEG)
            top = functools.reduce(jnp.maximum, pieces)
            old = row_max[h]
            new = jnp.maximum(old, jnp.max(top, axis=1, keepdims=True))
            shrink = jnp.exp2((old - new) * POW)
            weights = [jnp.exp2((piece - new) * POW) for piece in pieces]
            row_max[h] = new
            row_sum[h] = row_sum[h] * shrink + functools.reduce(jnp.add, weights)
            weights = jnp.concatenate([w.astype(jnp.bfloat16) for w in weights], axis=1)
            acc[h] = acc[h] * shrink + jnp.dot(weights, values, preferred_element_type=jnp.float32)

    head_units = heads // UNIT_HEADS
    units = tiles * head_units
    segments = 4

    def live(c):
        return (c >= 0) & (c < chunks)

    def first_hop(c):
        await_arrival(c, 0, 1)
        start(c, 2, 3, 5, 6)

        @pl.when(c + AHEAD < chunks)
        def _():
            start(c + AHEAD, 0, 1, 4)

    def second_hop(c):
        await_arrival(c, 2, 3)
        start(c, 7)

    def project_and_pair(c):
        await_arrival(c, 4, 5, 6, 7)
        project(c)
        start(c, 8, 9)

    def first_stage(c):
        await_arrival(c, 8, 9)
        start(c, 10, 11, 12, 13, 14, 15)

        @pl.when(c == 0)
        def _():
            meta_await(0)
            meta_start(1, 2, 3)

    def second_stage(c):
        await_arrival(c, 10, 11, 12, 13, 14, 15)
        start(c, 16, 17, 18, 19, 20, 21)

        @pl.when(c == 0)
        def _():
            meta_await(1, 2, 3)
            meta_start(4, 5, 6)

    def gathered(c):
        await_arrival(c, 16, 17, 18, 19, 20, 21)

        @pl.when(c == 0)
        def _():
            meta_await(4, 5, 6)
            find_pages()

    plan = (
        (0, 2, project_and_pair),
        (0, LAG, gathered),
        (0, 0, first_hop),
        (0, 3, first_stage),
        (2, 1, second_hop),
        (2, 4, second_stage),
    )

    for copy in own_hidden + weights_in + query_in + resident_in:
        copy.wait()

    def segment(g, carry):
        period, seg = g // segments, g % segments
        ready = period - LAG

        for at, lag, handler in plan:

            @pl.when((seg == at) & live(period - lag))
            def _(handler=handler, lag=lag):
                handler(period - lag)

        @pl.when(g == (LAG + 1) * segments)
        def _():
            page_copy.start()

        @pl.when(g == 1)
        def _():
            lax.fori_loop(0, count_full.shape[0] // tile_pages, count_pages, 0)

        @pl.when((g >= 4) & (g < 4 + pool // tile_pages))
        def _():
            resident_tile(g - 4)

        beat = ready - (GROUP - 1)

        @pl.when((beat >= 0) & (beat < chunks))
        def _():
            group = beat // GROUP * GROUP
            stage = beat % GROUP * segments + seg
            stages = GROUP * segments

            def one(u, inner):
                kt, hp = u // head_units, u % head_units

                @pl.when(kt < own_tile)
                def _():
                    attend(group, kt, hp, False)

                @pl.when(kt == own_tile)
                def _():
                    attend(group, kt, hp, True)

                return inner

            lax.fori_loop(stage * units // stages, (stage + 1) * units // stages, one, 0)

        return carry

    lax.fori_loop(0, (chunks + LAG + GROUP - 1) * segments, segment, 0)

    decode_incoming()
    for h in range(heads):
        total = jnp.sum(row_sum[h], axis=1, keepdims=True)
        out[:, h * lanes : (h + 1) * lanes] = (acc[h] / total).astype(out.dtype)
    decoded = jnp.transpose(dec_acc[...] / dec_sum[...])
    for h in range(heads):
        decode_out[:, h * lanes : (h + 1) * lanes] = decoded[
            h * decode_rows : (h + 1) * decode_rows, :
        ].astype(decode_out.dtype)

    def drain(c, carry):
        for g in range(len(GROUPS)):
            whole(c, g).wait_send()
        return carry

    lax.fori_loop(0, chunks, drain, 0)
    for k in range(N_META):
        meta_copy(k).wait_send()


def per_device(
    prefill_hidden,
    norm_gain,
    key_weight,
    value_weight,
    prefill_query,
    resident_keys,
    resident_values,
    decode_query,
    page_owner,
    block_table,
    context_len,
):
    stretch, width = prefill_hidden.shape
    heads = prefill_query.shape[1] // HD
    pool = resident_keys.shape[0]
    features = key_weight.shape[0]
    rows = stretch // CHUNKS
    tables = [jnp.asarray(each) for each in rope_tables(stretch, 32)]
    anywhere = pl.BlockSpec(memory_space=pl.ANY)
    vmem = pl.BlockSpec(memory_space=pltpu.VMEM)
    smem = pl.BlockSpec(memory_space=pltpu.SMEM)
    f32, bf16, i32 = jnp.float32, jnp.bfloat16, jnp.int32
    return pl.pallas_call(
        kernel,
        out_shape=(
            jax.ShapeDtypeStruct(prefill_query.shape, bf16),
            jax.ShapeDtypeStruct(decode_query.shape, bf16),
        ),
        in_specs=[
            anywhere,
            vmem,
            anywhere,
            anywhere,
            anywhere,
            anywhere,
            anywhere,
            vmem,
            smem,
            smem,
            smem,
            vmem,
            vmem,
            vmem,
            vmem,
        ],
        out_specs=(vmem, vmem),
        scratch_shapes=[
            pltpu.VMEM((CHUNKS, features // width, rows, width), bf16),
            pltpu.VMEM((features, 2 * HD), bf16),
            pltpu.VMEM((CHUNKS, 2, 4, 4, rows, HD), bf16),
            pltpu.VMEM((CHUNKS, 2, 4, 4, rows, HD), bf16),
            pltpu.VMEM((2, 4, 4, stretch // PAGE, HD), i32),
            pltpu.VMEM((heads, stretch, HD), bf16),
            pltpu.VMEM((pool, PAGE, HD), bf16),
            pltpu.VMEM((pool, PAGE, HD), bf16),
            pltpu.VMEM((heads * decode_query.shape[0], HD), bf16),
            pltpu.VMEM((stretch, HD), f32),
            pltpu.VMEM((stretch, HD), f32),
            pltpu.VMEM((heads, stretch, HD), f32),
            pltpu.VMEM((heads, stretch, HD), f32),
            pltpu.VMEM((heads, stretch, HD), f32),
            pltpu.VMEM((block_table.shape[1], HD), i32),
            pltpu.VMEM((1, HD), i32),
            pltpu.VMEM((pool + 64, HD), f32),
            pltpu.VMEM((pool + 64, HD), f32),
            pltpu.VMEM((2, HD), i32),
            pltpu.SMEM((2, HD), i32),
            pltpu.VMEM((1, HD), f32),
            pltpu.VMEM((1, HD), f32),
            pltpu.VMEM((HD, HD), f32),
            pltpu.SemaphoreType.DMA((CHUNKS + 5 + heads,)),
            pltpu.SemaphoreType.DMA((CHUNKS, len(GROUPS))),
            pltpu.SemaphoreType.DMA((CHUNKS, len(GROUPS))),
            pltpu.SemaphoreType.DMA((N_META,)),
            pltpu.SemaphoreType.DMA((N_META,)),
        ],
        compiler_params=pltpu.CompilerParams(
            collective_id=0, has_side_effects=True, vmem_limit_bytes=60 * 1024 * 1024
        ),
        name="attention_layer",
    )(
        prefill_hidden,
        norm_gain.reshape(1, features),
        key_weight,
        value_weight,
        prefill_query,
        resident_keys,
        resident_values,
        decode_query,
        page_owner,
        block_table,
        context_len,
        *tables,
    )


def solution(mesh):
    return jax.shard_map(
        per_device,
        mesh=mesh,
        in_specs=(
            P("section", "tp"),
            P(),
            P(None, "tp"),
            P(None, "tp"),
            P("section", "tp"),
            P("section", None, "tp"),
            P("section", None, "tp"),
            P("section", "tp"),
            P("section"),
            P("section", None),
            P("section"),
        ),
        out_specs=(P("section", "tp"), P("section", "tp")),
        check_vma=False,
    )
```

```python
import functools
import math

import numpy as np

import jax
import jax.numpy as jnp
from jax import lax
from jax.experimental import pallas as pl
from jax.experimental.pallas import tpu as pltpu
from jax.sharding import PartitionSpec as P

MESH = pl.DeviceIdType.MESH
HD = 128
PAGE = 16
NORM_EPSILON = 1e-05
ROPE_THETA = 500000.0
NEG = -1e30
CHUNKS = 8
TILE_Y = 4
UNIT_HEADS = 8
GROUP = 2
LAG = 6
AHEAD = 2
GROUPS = ((0, 1), (2, 3), (4, 5, 6, 7), (8, 9), (10, 11, 12, 13, 14, 15), (16, 17, 18, 19, 20, 21))
GROUP_OF = tuple(g for g, ks in enumerate(GROUPS) for _ in ks)
N_META = 7
POW = math.log2(math.e) / math.sqrt(HD)

NT = (((1,), (1,)), ((), ()))
TN = (((0,), (0,)), ((), ()))


def rope_tables(stretch, sections):
    half = HD // 2
    exponent = np.arange(half, dtype=np.float32) * np.float32(-2.0 * math.log(ROPE_THETA) / HD)
    frequency = np.exp(exponent).astype(np.float64)
    inner = np.arange(stretch)[:, None] * frequency[None, :]
    outer = (np.arange(sections) * stretch)[:, None] * frequency[None, :]

    def both(angles):
        cosine = np.concatenate([np.cos(angles), np.cos(angles)], axis=1)
        sine = np.concatenate([np.sin(angles), np.sin(angles)], axis=1)
        return cosine.astype(np.float32), sine.astype(np.float32)

    return both(inner) + both(outer)


def kernel(
    hidden,
    gain,
    key_weight,
    value_weight,
    query,
    resident_keys,
    resident_values,
    decode_query,
    owner,
    table,
    context,
    cos_in,
    sin_in,
    cos_out,
    sin_out,
    out,
    decode_out,
    hid,
    wkv,
    kb,
    vb,
    meta,
    qs,
    rk,
    rv,
    dqm,
    cosine,
    sine,
    row_max,
    row_sum,
    acc,
    visible_pages,
    last_page,
    count_full,
    count_last,
    slot_page,
    slot_index,
    dec_max,
    dec_sum,
    dec_acc,
    local_sem,
    send_sem,
    recv_sem,
    meta_send,
    meta_recv,
):
    stretch = hidden.shape[0]
    width = hidden.shape[1]
    chunks = kb.shape[0]
    rows = stretch // chunks
    half_rows = rows // 2
    heads = qs.shape[0]
    pages_chunk = rows // PAGE
    pages_here = stretch // PAGE
    pool = rk.shape[0]
    max_pages = table.shape[1]
    decode_rows = decode_query.shape[0]
    lanes = 128

    s = lax.axis_index("section")
    t = lax.axis_index("tp")
    zh, core = t // 2, t % 2
    zl, y, x = s // 16, (s // 4) % 4, s % 4
    t_r, t_l, t_o = ((zh + 1) % 4) * 2 + core, ((zh + 3) % 4) * 2 + core, ((zh + 2) % 4) * 2 + core
    other = 1 - core
    t_p = zh * 2 + other
    xp, xm, xo = (x + 1) % 4, (x + 3) % 4, (x + 2) % 4
    yp, ym, yo = (y + 1) % 4, (y + 3) % 4, (y + 2) % 4
    zo = 1 - zl

    def at_section(zz, yy, xx):
        return (zz * 16 + yy * 4 + xx, t)

    z_right, z_left, partner = (s, t_r), (s, t_l), (s, t_p)
    z_other = at_section(zo, y, x)
    x_right, x_left = at_section(zl, y, xp), at_section(zl, y, xm)
    y_up, y_down = at_section(zl, yp, x), at_section(zl, ym, x)
    x_far, y_far = at_section(zl, y, xo), at_section(zl, yo, x)

    def routes(c):
        top, bottom = pl.ds(0, half_rows), pl.ds(half_rows, half_rows)
        mine = hidden.at[pl.ds(pl.multiple_of(c * rows, rows), rows), :]
        return (
            (mine, hid.at[c, t], z_right),
            (mine, hid.at[c, t], z_left),
            (hid.at[c, t_l, top], hid.at[c, t_l, top], z_right),
            (hid.at[c, t_r, bottom], hid.at[c, t_r, bottom], z_left),
            (mine, hid.at[c, t], partner),
            (hid.at[c, t_l], hid.at[c, t_l], partner),
            (hid.at[c, t_r], hid.at[c, t_r], partner),
            (hid.at[c, t_o], hid.at[c, t_o], partner),
            (kb.at[c, zl, y, x], kb.at[c, zl, y, x], z_other),
            (vb.at[c, zl, y, x], vb.at[c, zl, y, x], z_other),
            (kb.at[c, :, y, x], kb.at[c, :, y, x], x_right),
            (kb.at[c, :, y, x], kb.at[c, :, y, x], x_left),
            (kb.at[c, :, y, x], kb.at[c, :, y, x], x_far),
            (vb.at[c, :, y, x], vb.at[c, :, y, x], y_up),
            (vb.at[c, :, y, x], vb.at[c, :, y, x], y_down),
            (vb.at[c, :, y, x], vb.at[c, :, y, x], y_far),
            (kb.at[c, :, y], kb.at[c, :, y], y_up),
            (kb.at[c, :, y], kb.at[c, :, y], y_down),
            (kb.at[c, :, y], kb.at[c, :, y], y_far),
            (vb.at[c, :, :, x], vb.at[c, :, :, x], x_right),
            (vb.at[c, :, :, x], vb.at[c, :, :, x], x_left),
            (vb.at[c, :, :, x], vb.at[c, :, :, x], x_far),
        )

    meta_routes = (
        (meta.at[zl, y, x], meta.at[zo, y, x], z_other),
        (meta.at[:, y, x], meta.at[:, y, xm], x_right),
        (meta.at[:, y, x], meta.at[:, y, xp], x_left),
        (meta.at[:, y, x], meta.at[:, y, xo], x_far),
        (meta.at[:, y], meta.at[:, ym], y_up),
        (meta.at[:, y], meta.at[:, yp], y_down),
        (meta.at[:, y], meta.at[:, yo], y_far),
    )

    def remote(c, k):
        source, target, device = routes(c)[k]
        return pltpu.make_async_remote_copy(
            src_ref=source,
            dst_ref=target,
            send_sem=send_sem.at[c, GROUP_OF[k]],
            recv_sem=recv_sem.at[c, GROUP_OF[k]],
            device_id=device,
            device_id_type=MESH,
        )

    def whole(c, g):
        view = (
            hid.at[c, pl.ds(0, 2)],
            hid.at[c, 0],
            hid.at[c, pl.ds(0, 4)],
            kb.at[c, 0, 0, pl.ds(0, 2)],
            kb.at[c, 0, pl.ds(0, 3)],
            hid.at[c, pl.ds(0, 6)],
        )[g]
        return pltpu.make_async_remote_copy(
            src_ref=view,
            dst_ref=view,
            send_sem=send_sem.at[c, g],
            recv_sem=recv_sem.at[c, g],
            device_id=partner,
            device_id_type=MESH,
        )

    def start(c, *ks):
        for k in ks:
            remote(c, k).start()

    def await_arrival(c, *ks):
        g = GROUP_OF[ks[0]]
        assert GROUPS[g] == ks
        whole(c, g).wait_recv()

    def meta_copy(k):
        source, _, device = meta_routes[k]
        return pltpu.make_async_remote_copy(
            src_ref=source,
            dst_ref=source,
            send_sem=meta_send.at[k],
            recv_sem=meta_recv.at[k],
            device_id=device,
            device_id_type=MESH,
        )

    def meta_arrival(k):
        _, landing, device = meta_routes[k]
        return pltpu.make_async_remote_copy(
            src_ref=landing,
            dst_ref=landing,
            send_sem=meta_send.at[k],
            recv_sem=meta_recv.at[k],
            device_id=device,
            device_id_type=MESH,
        )

    def meta_start(*ks):
        for k in ks:
            meta_copy(k).start()

    def meta_await(*ks):
        for k in ks:
            meta_arrival(k).wait_recv()

    own_hidden = [
        pltpu.make_async_copy(
            hidden.at[pl.ds(c * rows, rows), :], hid.at[c, t], local_sem.at[c]
        )
        for c in range(chunks)
    ]
    weights_in = [
        pltpu.make_async_copy(key_weight, wkv.at[:, pl.ds(0, lanes)], local_sem.at[chunks]),
        pltpu.make_async_copy(value_weight, wkv.at[:, pl.ds(lanes, lanes)], local_sem.at[chunks + 1]),
    ]
    resident_in = [
        pltpu.make_async_copy(resident_keys, rk, local_sem.at[chunks + 2]),
        pltpu.make_async_copy(resident_values, rv, local_sem.at[chunks + 3]),
    ]
    query_in = [
        pltpu.make_async_copy(
            query.at[:, pl.ds(h * lanes, lanes)], qs.at[h], local_sem.at[chunks + 4 + h]
        )
        for h in range(heads)
    ]

    neighbours = (
        z_right,
        z_left,
        partner,
        z_other,
        x_right,
        x_left,
        x_far,
        y_up,
        y_down,
        y_far,
    )
    barrier = pltpu.get_barrier_semaphore()
    for device in neighbours:
        pl.semaphore_signal(barrier, inc=1, device_id=device, device_id_type=MESH)
    pl.semaphore_wait(barrier, len(neighbours))
    for c in range(AHEAD):
        start(c, 0, 1, 4)
    for copy in own_hidden + resident_in + weights_in + query_in:
        copy.start()

    owners = [owner[i] for i in range(pages_here)]
    page_row = lax.broadcasted_iota(jnp.int32, (pages_here, lanes), 0)
    codes = jnp.zeros((pages_here, lanes), jnp.int32)
    for i in range(pages_here):
        rank = jnp.int32(0)
        for j in range(i):
            rank = rank + jnp.where(owners[j] == owners[i], 1, 0).astype(jnp.int32)
        code = owners[i] * (count_full.shape[0] - pool) + s * 2 + rank
        codes = jnp.where(page_row == i, code, codes)
    meta[zl, y, x] = codes

    lane_row = lax.broadcasted_iota(jnp.int32, (1, lanes), 1) % decode_rows
    lengths = jnp.zeros((1, lanes), jnp.int32)
    for r in range(decode_rows):
        lengths = jnp.where(lane_row == r, context[r], lengths)
    full_pages = lax.shift_right_logical(lengths - 1, 4)
    last_tokens = lengths - full_pages * PAGE
    last_page[...] = jnp.zeros((1, lanes), jnp.int32)

    def table_row(j, carry):
        entries = jnp.zeros((1, lanes), jnp.int32)
        for r in range(decode_rows):
            entries = jnp.where(lane_row == r, table[r, j], entries)
        visible_pages[pl.ds(j, 1), :] = jnp.where(full_pages > j, entries, -1)
        last_page[...] = jnp.where(full_pages == j, entries, last_page[...])
        return carry

    lax.fori_loop(0, max_pages, table_row, 0)
    meta_start(0)

    for h in range(heads):
        dqm[h * decode_rows : (h + 1) * decode_rows, :] = decode_query[:, h * lanes : (h + 1) * lanes]
    ca, sa = cos_out[pl.ds(s, 1), :], sin_out[pl.ds(s, 1), :]
    low = lax.broadcasted_iota(jnp.int32, (1, lanes), 1) < lanes // 2
    cosine[...] = ca * cos_in[...] - sa * sin_in[...]
    sine[...] = jnp.where(low, -1.0, 1.0) * (sa * cos_in[...] + ca * sin_in[...])
    row_max[...] = jnp.full(row_max.shape, NEG, jnp.float32)
    row_sum[...] = jnp.zeros(row_sum.shape, jnp.float32)
    acc[...] = jnp.zeros(acc.shape, jnp.float32)
    dec_max[...] = jnp.full(dec_max.shape, NEG, jnp.float32)
    dec_sum[...] = jnp.zeros(dec_sum.shape, jnp.float32)
    dec_acc[...] = jnp.zeros(dec_acc.shape, jnp.float32)

    tile_pages = 32

    def count_pages(i, carry):
        first = pl.multiple_of(i * tile_pages, tile_pages)
        ids = first + lax.broadcasted_iota(jnp.int32, (tile_pages, lanes), 0)

        def step(j, total):
            return total + jnp.where(ids == visible_pages[pl.ds(j, 1), :], 1.0, 0.0)

        count_full[pl.ds(first, tile_pages), :] = lax.fori_loop(
            0, max_pages, step, jnp.zeros(ids.shape, jnp.float32), unroll=8
        )
        count_last[pl.ds(first, tile_pages), :] = jnp.where(ids == last_page[...], 1.0, 0.0)
        return carry

    slots = count_full.shape[0] - pool

    def decode_tile(keys, values, counts):
        scores = lax.dot_general(keys, dqm[...], NT, preferred_element_type=jnp.float32)
        scores = jnp.where(counts > 0.0, scores, NEG)
        old = dec_max[...]
        new = jnp.maximum(old, jnp.max(scores, axis=0, keepdims=True))
        weights = counts * jnp.exp2((scores - new) * POW)
        shrink = jnp.exp2((old - new) * POW)
        dec_max[...] = new
        dec_sum[...] = dec_sum[...] * shrink + jnp.sum(weights, axis=0, keepdims=True)
        dec_acc[...] = dec_acc[...] * shrink + lax.dot_general(
            values, weights.astype(jnp.bfloat16), TN, preferred_element_type=jnp.float32
        )

    token_of = lax.broadcasted_iota(jnp.int32, (PAGE, lanes), 0)
    in_last = jnp.where(token_of < last_tokens, 1.0, 0.0)

    def token_counts(full, last):
        return jnp.broadcast_to(full, (PAGE, lanes)) + in_last * jnp.broadcast_to(
            last, (PAGE, lanes)
        )

    def resident_tile(i):
        first = pl.multiple_of(i * tile_pages, tile_pages)
        full = count_full[pl.ds(first, tile_pages), :]
        last = count_last[pl.ds(first, tile_pages), :]
        counts = [token_counts(full[p : p + 1], last[p : p + 1]) for p in range(tile_pages)]
        decode_tile(
            rk[pl.ds(first, tile_pages)].reshape(tile_pages * PAGE, lanes),
            rv[pl.ds(first, tile_pages)].reshape(tile_pages * PAGE, lanes),
            jnp.concatenate(counts, axis=0),
        )

    page_copy = pltpu.make_async_copy(slot_page, slot_index, local_sem.at[chunks + 4 + heads])

    def find_pages():
        lane = lax.broadcasted_iota(jnp.int32, (pages_here, lanes), 1)
        found = jnp.zeros((pages_here, lanes), jnp.int32)
        for i in range(32):
            here = (meta[i // 16, i // 4 % 4, i % 4] == s * slots + lane) & (lane // 2 == i)
            found = found + jnp.where(here, page_row, 0)
        page = jnp.minimum(jnp.sum(found, axis=0, keepdims=True), pages_here - 1)
        slot_page[0:1, :] = page // pages_chunk
        slot_page[1:2, :] = page % pages_chunk

    def decode_incoming():
        page_copy.wait()

        def fetch(k, carry):
            sec = k // 2
            chunk, page = slot_index[0, k], slot_index[1, k]
            keys = kb[chunk, sec // 16, sec // 4 % 4, sec % 4]
            values = vb[chunk, sec // 16, sec // 4 % 4, sec % 4]
            first, second = keys[:PAGE], values[:PAGE]
            for p in range(1, pages_chunk):
                part = slice(p * PAGE, (p + 1) * PAGE)
                first = jnp.where(page == p, keys[part], first)
                second = jnp.where(page == p, values[part], second)
            rk[k] = first
            rv[k] = second
            return carry

        lax.fori_loop(0, slots, fetch, 0, unroll=4)
        full, last = count_full[pool:, :], count_last[pool:, :]
        counts = [token_counts(full[p : p + 1], last[p : p + 1]) for p in range(slots)]
        decode_tile(
            rk[:slots].reshape(slots * PAGE, lanes),
            rv[:slots].reshape(slots * PAGE, lanes),
            jnp.concatenate(counts, axis=0),
        )

    shards = hid.shape[1]

    def project(c):
        squares = jnp.zeros((rows, 1), jnp.float32)
        for j in range(shards):
            block = hid[c, j].astype(jnp.float32)
            squares = squares + jnp.sum(block * block, axis=1, keepdims=True)
        inverse = lax.rsqrt(squares * (1.0 / (shards * width)) + NORM_EPSILON)
        total = jnp.zeros((rows, 2 * lanes), jnp.float32)
        for j in range(shards):
            block = hid[c, j].astype(jnp.float32)
            normed = (block * inverse * gain[:, j * width : (j + 1) * width]).astype(jnp.bfloat16)
            total = total + jnp.dot(
                normed, wkv[j * width : (j + 1) * width, :], preferred_element_type=jnp.float32
            )
        keys = total[:, :lanes]
        at = pl.ds(pl.multiple_of(c * rows, rows), rows)
        keys = keys * cosine[at, :] + pltpu.roll(keys, lanes // 2, 1) * sine[at, :]
        kb[c, zl, y, x] = keys.astype(jnp.bfloat16)
        vb[c, zl, y, x] = total[:, lanes:].astype(jnp.bfloat16)

    tile_sections = 4 * TILE_Y
    tile_keys = GROUP * tile_sections * rows
    tiles = 32 // tile_sections
    own_tile = s // tile_sections

    def attend(c, kt, hp, masked):
        first_y = kt * TILE_Y
        at = (pl.ds(c, GROUP), first_y // 4, pl.ds(first_y % 4, TILE_Y))
        keys = kb[at].reshape(tile_keys, lanes)
        values = vb[at].reshape(tile_keys, lanes)
        if masked:
            n = lax.broadcasted_iota(jnp.int32, (1, lanes), 1)
            query_pos = s * stretch + lax.broadcasted_iota(jnp.int32, (stretch, lanes), 0)
        def score(i):
            return lax.dot_general(
                qs[hp * UNIT_HEADS + i], keys, NT, preferred_element_type=jnp.float32
            )

        following = score(0)
        for i in range(UNIT_HEADS):
            h = hp * UNIT_HEADS + i
            scores = following
            if i + 1 < UNIT_HEADS:
                following = score(i + 1)
            pieces = [scores[:, j * lanes : (j + 1) * lanes] for j in range(tile_keys // lanes)]
            if masked:
                for j in range(len(pieces)):
                    at = j * lanes + n
                    part, rest = at // (tile_sections * rows), at % (tile_sections * rows)
                    key_pos = (kt * tile_sections + rest // rows) * stretch
                    key_pos = key_pos + (c + part) * rows + rest % rows
                    pieces[j] = jnp.where(key_pos <= query_pos, pieces[j], NEG)
            top = functools.reduce(jnp.maximum, pieces)
            old = row_max[h]
            new = jnp.maximum(old, jnp.max(top, axis=1, keepdims=True))
            shrink = jnp.exp2((old - new) * POW)
            weights = [jnp.exp2((piece - new) * POW) for piece in pieces]
            row_max[h] = new
            row_sum[h] = row_sum[h] * shrink + functools.reduce(jnp.add, weights)
            weights = jnp.concatenate([w.astype(jnp.bfloat16) for w in weights], axis=1)
            acc[h] = acc[h] * shrink + jnp.dot(weights, values, preferred_element_type=jnp.float32)

    head_units = heads // UNIT_HEADS
    units = tiles * head_units
    segments = 4

    def live(c):
        return (c >= 0) & (c < chunks)

    def first_hop(c):
        await_arrival(c, 0, 1)
        start(c, 2, 3, 5, 6)

        @pl.when(c + AHEAD < chunks)
        def _():
            start(c + AHEAD, 0, 1, 4)

    def second_hop(c):
        await_arrival(c, 2, 3)
        start(c, 7)

    def project_and_pair(c):
        await_arrival(c, 4, 5, 6, 7)
        project(c)
        start(c, 8, 9)

    def first_stage(c):
        await_arrival(c, 8, 9)
        start(c, 10, 11, 12, 13, 14, 15)

        @pl.when(c == 0)
        def _():
            meta_await(0)
            meta_start(1, 2, 3)

    def second_stage(c):
        await_arrival(c, 10, 11, 12, 13, 14, 15)
        start(c, 16, 17, 18, 19, 20, 21)

        @pl.when(c == 0)
        def _():
            meta_await(1, 2, 3)
            meta_start(4, 5, 6)

    def gathered(c):
        await_arrival(c, 16, 17, 18, 19, 20, 21)

        @pl.when(c == 0)
        def _():
            meta_await(4, 5, 6)
            find_pages()

    plan = (
        (0, 2, project_and_pair),
        (0, LAG, gathered),
        (0, 0, first_hop),
        (0, 3, first_stage),
        (2, 1, second_hop),
        (2, 4, second_stage),
    )

    for copy in own_hidden + weights_in + query_in + resident_in:
        copy.wait()

    def segment(g, carry):
        period, seg = g // segments, g % segments
        ready = period - LAG

        for at, lag, handler in plan:

            @pl.when((seg == at) & live(period - lag))
            def _(handler=handler, lag=lag):
                handler(period - lag)

        @pl.when(g == (LAG + 1) * segments)
        def _():
            page_copy.start()

        @pl.when(g == 1)
        def _():
            lax.fori_loop(0, count_full.shape[0] // tile_pages, count_pages, 0)

        @pl.when((g >= 4) & (g < 4 + pool // tile_pages))
        def _():
            resident_tile(g - 4)

        beat = ready - (GROUP - 1)

        @pl.when((beat >= 0) & (beat < chunks))
        def _():
            group = beat // GROUP * GROUP
            stage = beat % GROUP * segments + seg
            stages = GROUP * segments

            def one(u, inner):
                kt, hp = u // head_units, u % head_units

                @pl.when(kt < own_tile)
                def _():
                    attend(group, kt, hp, False)

                @pl.when(kt == own_tile)
                def _():
                    attend(group, kt, hp, True)

                return inner

            lax.fori_loop(stage * units // stages, (stage + 1) * units // stages, one, 0)

        return carry

    lax.fori_loop(0, (chunks + LAG + GROUP - 1) * segments, segment, 0)

    decode_incoming()
    for h in range(heads):
        total = jnp.sum(row_sum[h], axis=1, keepdims=True)
        out[:, h * lanes : (h + 1) * lanes] = (acc[h] / total).astype(out.dtype)
    decoded = jnp.transpose(dec_acc[...] / dec_sum[...])
    for h in range(heads):
        decode_out[:, h * lanes : (h + 1) * lanes] = decoded[
            h * decode_rows : (h + 1) * decode_rows, :
        ].astype(decode_out.dtype)

    def drain(c, carry):
        for g in range(len(GROUPS)):
            whole(c, g).wait_send()
        return carry

    lax.fori_loop(0, chunks, drain, 0)
    for k in range(N_META):
        meta_copy(k).wait_send()


def store(prefill, decode, prefill_out, decode_out):
    prefill_out[...] = prefill[...]
    decode_out[...] = decode[...]


def per_device(
    prefill_hidden,
    norm_gain,
    key_weight,
    value_weight,
    prefill_query,
    resident_keys,
    resident_values,
    decode_query,
    page_owner,
    block_table,
    context_len,
):
    stretch, width = prefill_hidden.shape
    heads = prefill_query.shape[1] // HD
    pool = resident_keys.shape[0]
    features = key_weight.shape[0]
    rows = stretch // CHUNKS
    tables = [jnp.asarray(each) for each in rope_tables(stretch, 32)]
    anywhere = pl.BlockSpec(memory_space=pl.ANY)
    vmem = pl.BlockSpec(memory_space=pltpu.VMEM)
    smem = pl.BlockSpec(memory_space=pltpu.SMEM)
    f32, bf16, i32 = jnp.float32, jnp.bfloat16, jnp.int32
    attended = pl.pallas_call(
        kernel,
        out_shape=(
            jax.ShapeDtypeStruct(prefill_query.shape, bf16),
            jax.ShapeDtypeStruct(decode_query.shape, bf16),
        ),
        in_specs=[
            anywhere,
            vmem,
            anywhere,
            anywhere,
            anywhere,
            anywhere,
            anywhere,
            vmem,
            smem,
            smem,
            smem,
            vmem,
            vmem,
            vmem,
            vmem,
        ],
        out_specs=(vmem, vmem),
        scratch_shapes=[
            pltpu.VMEM((CHUNKS, features // width, rows, width), bf16),
            pltpu.VMEM((features, 2 * HD), bf16),
            pltpu.VMEM((CHUNKS, 2, 4, 4, rows, HD), bf16),
            pltpu.VMEM((CHUNKS, 2, 4, 4, rows, HD), bf16),
            pltpu.VMEM((2, 4, 4, stretch // PAGE, HD), i32),
            pltpu.VMEM((heads, stretch, HD), bf16),
            pltpu.VMEM((pool, PAGE, HD), bf16),
            pltpu.VMEM((pool, PAGE, HD), bf16),
            pltpu.VMEM((heads * decode_query.shape[0], HD), bf16),
            pltpu.VMEM((stretch, HD), f32),
            pltpu.VMEM((stretch, HD), f32),
            pltpu.VMEM((heads, stretch, HD), f32),
            pltpu.VMEM((heads, stretch, HD), f32),
            pltpu.VMEM((heads, stretch, HD), f32),
            pltpu.VMEM((block_table.shape[1], HD), i32),
            pltpu.VMEM((1, HD), i32),
            pltpu.VMEM((pool + 64, HD), f32),
            pltpu.VMEM((pool + 64, HD), f32),
            pltpu.VMEM((2, HD), i32),
            pltpu.SMEM((2, HD), i32),
            pltpu.VMEM((1, HD), f32),
            pltpu.VMEM((1, HD), f32),
            pltpu.VMEM((HD, HD), f32),
            pltpu.SemaphoreType.DMA((CHUNKS + 5 + heads,)),
            pltpu.SemaphoreType.DMA((CHUNKS, len(GROUPS))),
            pltpu.SemaphoreType.DMA((CHUNKS, len(GROUPS))),
            pltpu.SemaphoreType.DMA((N_META,)),
            pltpu.SemaphoreType.DMA((N_META,)),
        ],
        compiler_params=pltpu.CompilerParams(
            collective_id=0, has_side_effects=True, vmem_limit_bytes=60 * 1024 * 1024
        ),
        name="attention_layer",
    )(
        prefill_hidden,
        norm_gain.reshape(1, features),
        key_weight,
        value_weight,
        prefill_query,
        resident_keys,
        resident_values,
        decode_query,
        page_owner,
        block_table,
        context_len,
        *tables,
    )
    return pl.pallas_call(
        store,
        out_shape=tuple(jax.ShapeDtypeStruct(each.shape, each.dtype) for each in attended),
        in_specs=[vmem, vmem],
        out_specs=(vmem, vmem),
        name="store",
    )(*attended)


def solution(mesh):
    return jax.shard_map(
        per_device,
        mesh=mesh,
        in_specs=(
            P("section", "tp"),
            P(),
            P(None, "tp"),
            P(None, "tp"),
            P("section", "tp"),
            P("section", None, "tp"),
            P("section", None, "tp"),
            P("section", "tp"),
            P("section"),
            P("section", None),
            P("section"),
        ),
        out_specs=(P("section", "tp"), P("section", "tp")),
        check_vma=False,
    )
```
